128 devices in a mesh: pb: 16 (over x, z_lo, core), kv: 8 (over z_hi, y).
Axes of the slice: x: 4, y: 4, z: 4 (z_hi: 2, z_lo: 2; z = z_hi * 2 + z_lo), core: 2. Of those that a mesh axis runs over, the one named last changes fastest.
Arguments:
- queries: float32 [16384, 256], P(('pb', 'kv')), may hold values from -200 to 200
- keys: float32 [16384, 256], P(('pb', 'kv')), may hold values from -8 to 8
- values: float32 [16384, 256], P(('pb', 'kv')), may hold values from -192 to 192
- query_tangent: float32 [16384, 256], P(('pb', 'kv')), may hold values from -6 to 6
- key_tangent: float32 [16384, 256], P(('pb', 'kv')), may hold values from -6 to 6
- value_tangent: float32 [16384, 256], P(('pb', 'kv')), may hold values from -192 to 192
Outputs:
- attended: float32 [16384, 256], P(('pb', 'kv'))
- attended_tangent: float32 [16384, 256], P(('pb', 'kv'))
The draws below stay inside these ranges and needn't reach their ends.
All inputs are finite; a program needn't handle non-finite values.
Results may differ from the reference program's by a relative error of at most 0.0003.
Values sent between devices are 32-bit elements; how exact they have to be, the bound alone decides.
A program may use at most 128 MiB of HBM per device.

```python
import math
import jax
import jax.numpy as jnp
from jax import lax

DH = 128
HEADS = 2
WIDTH = 256
SEQ = 16384


def drawn_pair(key):
    shape = (SEQ, HEADS, DH)
    keys = jnp.clip(jax.random.normal(jax.random.fold_in(key, 11), shape, jnp.float32), -6.0, 6.0) * 1.2
    queries = jnp.clip(jax.random.normal(jax.random.fold_in(key, 12), shape, jnp.float32), -6.0, 6.0) * 1.2
    row_scale = jnp.exp(jax.random.uniform(jax.random.fold_in(key, 16), (SEQ, HEADS, 1), jnp.float32, 0.0, math.log(16.0)))
    queries = queries * row_scale
    return (queries.reshape(SEQ, HEADS * DH), keys.reshape(SEQ, HEADS * DH))


def draw_queries(key, part):
    return drawn_pair(key)[0]


def draw_keys(key, part):
    return drawn_pair(key)[1]


def level_of(rng, extent, split, smallest, high):
    factor_of, own = 1.0, jax.random.fold_in(rng, 6)
    for dim, shards_of in split:
        heights = jnp.exp(jax.random.uniform(jax.random.fold_in(own, dim), (shards_of,), jnp.float32, smallest / len(split), high / len(split)))
        factor_of = factor_of * jnp.repeat(heights, extent[dim] // shards_of).reshape([-1 if axis == dim else 1 for axis in range(len(extent))])
    return factor_of


def bell_draw(rng, dims, spread, reach, shards=(), held_as=jnp.bfloat16):
    result = spread * jax.random.normal(rng, dims, jnp.float32)
    if shards:
        result = result * level_of(rng, dims, shards, -0.22, 0.18)
    return jnp.clip(result, -reach, reach).astype(held_as)


def setup_inputs(seed: int = 0) -> dict:
    streams_of = jax.random.split(jax.random.key(seed), 7)
    return {
        "queries": draw_queries(jax.random.fold_in(streams_of[6], 71), 0),
        "keys": draw_keys(jax.random.fold_in(streams_of[6], 71), 0),
        "values": bell_draw(streams_of[2], (SEQ, WIDTH), 32.0, 192.0, ((0, 128),), jnp.float32),
        "query_tangent": bell_draw(streams_of[3], (SEQ, WIDTH), 1.0, 6.0, ((0, 128),), jnp.float32),
        "key_tangent": bell_draw(streams_of[4], (SEQ, WIDTH), 1.0, 6.0, ((0, 128),), jnp.float32),
        "value_tangent": bell_draw(streams_of[5], (SEQ, WIDTH), 32.0, 192.0, ((0, 128),), jnp.float32),
    }


def cross(left, right):
    return lax.dot_general(left, right, (((1,), (1,)), ((), ())), precision=lax.Precision.HIGHEST, preferred_element_type=jnp.float32)

def product(left, right):
    return jnp.dot(left, right, precision=lax.Precision.HIGHEST, preferred_element_type=jnp.float32)

def reference(queries, keys, values, query_tangent, key_tangent, value_tangent):
    total = queries.shape[0]
    block = min(1024, total)
    heads = queries.shape[1] // DH
    scale = 1.0 / math.sqrt(DH)
    outs = []
    tangents = []
    for head in range(heads):
        cols = slice(head * DH, (head + 1) * DH)
        key_h = keys[:, cols]
        val_h = values[:, cols]
        dkey_h = key_tangent[:, cols]
        dval_h = value_tangent[:, cols]
        q_blocks = queries[:, cols].reshape(total // block, block, DH)
        dq_blocks = query_tangent[:, cols].reshape(total // block, block, DH)

        def one_block(pair):
            q_rows, dq_rows = pair
            scores = cross(q_rows, key_h) * scale
            score_tangent = (cross(dq_rows, key_h) + cross(q_rows, dkey_h)) * scale
            peak = lax.optimization_barrier(jnp.max(scores, axis=1, keepdims=True))
            expo = jnp.exp(scores - peak)
            weights = expo / lax.optimization_barrier(jnp.sum(expo, axis=1, keepdims=True))
            mean_t = lax.optimization_barrier(jnp.sum(weights * score_tangent, axis=1, keepdims=True))
            attended = product(weights, val_h)
            tangent = product(weights * (score_tangent - mean_t), val_h) + product(weights, dval_h)
            return (attended, tangent)
        att, tan = lax.map(one_block, (q_blocks, dq_blocks))
        outs.append(att.reshape(total, DH))
        tangents.append(tan.reshape(total, DH))
    return (jnp.concatenate(outs, axis=1), jnp.concatenate(tangents, axis=1))
```

```python
import math

import jax
import jax.numpy as jnp
from jax import lax
from jax.experimental import pallas as pl
from jax.experimental.pallas import tpu as pltpu
from jax.sharding import PartitionSpec as P

DH = 128
LN = 256
F32, BF = jnp.float32, jnp.bfloat16
MESH = pl.DeviceIdType.MESH
ORDER = (0, 1, 2, 4, 3, 5, 6, 7)
POS = tuple(ORDER.index(r) for r in range(8))
THIRD = ((0, 88), (88, 88), (176, 80))
PART = ((0, 96), (96, 96), (192, 88))
STAT = (88, 184, 272)


def nt(a, b):
    return lax.dot_general(a, b, (((1,), (1,)), ((), ())), preferred_element_type=F32)


def nn(a, b):
    return jnp.dot(a, b, preferred_element_type=F32)


def two(x):
    hi = x.astype(BF)
    return hi, (x - hi.astype(F32)).astype(BF)


def three(x):
    hi = x.astype(BF)
    rest = x - hi.astype(F32)
    mid = rest.astype(BF)
    return hi, mid, (rest - mid.astype(F32)).astype(BF)


def kernel(q, dq, k, dk, v, dv, o, ot, kvb, qb, ks, ky, vh, vl, qs, qx, ac, rb, fin,
           swap_s, swap_r, own_s, ks_s, ks_r, qs_s, qs_r, b_s, b_r, f_s, f_r, f_o):
    pb, kv = lax.axis_index("pb"), lax.axis_index("kv")
    core, x = pb % 2, pb // 4
    z, y = (kv // 4) * 2 + (pb // 2) % 2, kv % 4

    def dev(x, y, z, c):
        return (x * 4 + (z % 2) * 2 + c, (z // 2) * 4 + y)

    def near(i):
        return i + 1 - 2 * (i % 2)

    def far(i):
        return (i + 2 * (i % 2) + 3) % 4

    kn = (dev(near(x), y, z, core), dev(x, near(y), z, core), dev(x, y, near(z), core))
    qn = (dev(far(x), y, z, core), dev(x, far(y), z, core), dev(x, y, far(z), core))
    sib = dev(x, y, z, 1 - core)

    barrier = pltpu.get_barrier_semaphore()
    for other in kn + qn + (sib,):
        pl.semaphore_signal(barrier, inc=1, device_id=other, device_id_type=MESH)
    pl.semaphore_wait(barrier, 7)

    mine = pl.ds(pl.multiple_of(core * DH, DH), DH)
    theirs = pl.ds(pl.multiple_of((1 - core) * DH, DH), DH)
    rows = pl.ds(pl.multiple_of(core * 128, 128), 128)
    swaps, owns = [], []
    for i, (ref, dst, a) in enumerate(
        ((q, qb, 0), (dq, qb, 1), (k, kvb, 0), (dk, kvb, 1), (v, kvb, 2), (dv, kvb, 3))
    ):
        swaps.append(pltpu.make_async_remote_copy(
            src_ref=ref.at[:, theirs], dst_ref=dst.at[a, 0, rows],
            send_sem=swap_s.at[i], recv_sem=swap_r.at[i], device_id=sib, device_id_type=MESH))
        owns.append(pltpu.make_async_copy(ref.at[:, mine], dst.at[a, 0, rows], own_s.at[i]))
    for c in swaps + owns:
        c.start()

    def route(buf, near_of, send, recv):
        def msg(t, to):
            dims = [(t + i) % 3 for i in range(3)]
            d = [i for i in dims if to >> i & 1][-1]
            part = pl.ds(*THIRD[t])
            return pltpu.make_async_remote_copy(
                src_ref=buf.at[:, POS[to ^ (1 << d)], part], dst_ref=buf.at[:, POS[to], part],
                send_sem=send.at[t * 8 + to], recv_sem=recv.at[t * 8 + to],
                device_id=near_of[d], device_id_type=MESH)
        return {(t, to): msg(t, to) for t in range(3) for to in range(1, 8)}

    kmsg, qmsg = route(kvb, kn, ks_s, ks_r), route(qb, qn, qs_s, qs_r)

    def names(t):
        return 1 << t, 1 << (t + 1) % 3, 1 << (t + 2) % 3

    def begin(m):
        for step in range(3):
            for t in range(3):
                m[t, names(t)[step]].start()

    def pass_first(m):
        for t in range(3):
            a, b, c = names(t)
            m[t, a].wait_recv()
            m[t, a | b].start()
            m[t, a | c].start()

    def pass_second(m):
        for t in range(3):
            a, b, c = names(t)
            m[t, b].wait_recv()
            m[t, b | c].start()

    def pass_both(m):
        for t in range(3):
            a, b, c = names(t)
            m[t, a | b].wait_recv()
            m[t, a | b | c].start()

    def end_near(m):
        for t in range(3):
            m[t, names(t)[2]].wait_recv()

    def end_far(m):
        for t in range(3):
            a, b, c = names(t)
            for to in (a | c, b | c, a | b | c):
                m[t, to].wait_recv()

    root = 1.0 / math.sqrt(DH)
    base2 = root * math.log2(math.e)

    def prep_k(first, count):
        def one(i, _):
            r = pl.ds(pl.multiple_of(i * LN, LN), LN)
            kh, km, kl = three(kvb[0, i])
            dh, dm = two(kvb[1, i])
            ks[r, :] = jnp.concatenate([kh, km, kh, km, kl, kh], axis=1)
            ky[r, :] = jnp.concatenate([kh, dh, km, dm, kh, dh], axis=1)
            for a in range(2):
                hi, lo = two(jnp.transpose(kvb[2 + a, i]))
                vh[a * DH:(a + 1) * DH, r] = hi
                vl[a * DH:(a + 1) * DH, r] = lo
            return 0
        lax.fori_loop(first, first + count, one, 0)

    def prep_q(first, count):
        def one(i, _):
            r = pl.ds(pl.multiple_of(i * LN, LN), LN)
            raw = qb[0, i]
            h, m, l = three(raw * base2)
            qs[r, :] = jnp.concatenate([h, h, m, m, h, l], axis=1)
            h, m = two(raw * root)
            dh, dm = two(qb[1, i] * root)
            qx[r, :] = jnp.concatenate([dh, h, dh, h, dm, m], axis=1)
            ac[i] = jnp.zeros(ac.shape[1:], F32)
            ac[i, 88:89, :] = jnp.full((1, LN), -1e30, F32)
            return 0
        lax.fori_loop(first, first + count, one, 0)

    def tile(first, count, k0, keys):
        r = pl.ds(pl.multiple_of(first * LN, LN), count * LN)
        c = slice(k0 * LN, k0 * LN + keys)

        def lanes(row):
            return jnp.concatenate([ac[first + i, row:row + 1, :] for i in range(count)], axis=1)

        s = nt(ks[c, :], qs[r, :])
        t = nt(ky[c, :], qx[r, :])
        old = lanes(88)
        peak = jnp.maximum(old, jnp.max(s, axis=0, keepdims=True))
        fade = jnp.exp2(old - peak)
        e = jnp.exp2(s - peak)
        w = e * t
        total = lanes(89) * fade + jnp.sum(e, axis=0, keepdims=True)
        total_t = lanes(90) * fade + jnp.sum(w, axis=0, keepdims=True)
        eh, el = two(e)
        wh, wl = two(w)
        hi, lo = vh[:, c], vl[:, c]
        n = nn(hi, eh) + nn(lo, eh) + nn(hi, el)
        u = nn(hi[:DH], wh) + nn(lo[:DH], wh) + nn(hi[:DH], wl)
        tan = n[DH:] + u
        for i in range(count):
            s_ = slice(i * LN, (i + 1) * LN)
            f = fade[:, s_]
            at = first + i
            ac[at, 0:88, :] = ac[at, 0:88, :] * f + n[0:88, s_]
            ac[at, 96:136, :] = ac[at, 96:136, :] * f + n[88:128, s_]
            ac[at, 136:184, :] = ac[at, 136:184, :] * f + tan[0:48, s_]
            ac[at, 192:272, :] = ac[at, 192:272, :] * f + tan[48:128, s_]
            ac[at, 88:89, :] = peak[:, s_]
            ac[at, 89:90, :] = total[:, s_]
            ac[at, 90:91, :] = total_t[:, s_]

    def sweep(first, tiles, count, k0, keys):
        def one(i, _):
            tile(first + i * count, count, k0, keys)
            return 0
        lax.fori_loop(0, tiles, one, 0)

    def bmsg(t, src, d, i, n_):
        r0, n = PART[t]
        return pltpu.make_async_remote_copy(
            src_ref=ac.at[POS[src], pl.ds(r0, n)], dst_ref=rb.at[t, i, pl.ds(0, n)],
            send_sem=b_s.at[t * 7 + i], recv_sem=b_r.at[t * 7 + i],
            device_id=qn[d], device_id_type=MESH)

    back = {}
    for t in range(3):
        a, b, c = names(t)
        for i, to in enumerate((0, a, b, a | b)):
            back[t, 1, to] = bmsg(t, to | c, (t + 2) % 3, i, 0)
        for i, to in enumerate((0, a)):
            back[t, 2, to] = bmsg(t, to | b, (t + 1) % 3, 4 + i, 0)
        back[t, 3, 0] = bmsg(t, a, t, 6, 0)

    def leave(pos):
        ac[pos, 184:192, :] = ac[pos, 88:96, :]
        ac[pos, 272:280, :] = ac[pos, 88:96, :]
        r = ORDER[pos]
        for t in range(3):
            c = names(t)[2]
            if r & c:
                back[t, 1, r ^ c].start()

    def merge(t, step, to):
        back[t, step, to].wait_recv()
        a, b, _ = names(t)
        i = {1: {0: 0, a: 1, b: 2, a | b: 3}, 2: {0: 4, a: 5}, 3: {0: 6}}[step][to]
        r0, n = PART[t]
        st, p = STAT[t], POS[to]
        m1, m2 = ac[p, st:st + 1, :], rb[t, i, n - 8:n - 7, :]
        top = jnp.maximum(m1, m2)
        f1, f2 = jnp.exp2(m1 - top), jnp.exp2(m2 - top)
        ac[p, r0:r0 + n, :] = ac[p, r0:r0 + n, :] * f1 + rb[t, i, :n, :] * f2
        ac[p, st:st + 1, :] = top

    for i in range(6):
        swaps[i].wait_recv()
        owns[i].wait()
    begin(qmsg)
    begin(kmsg)
    prep_k(0, 1)
    prep_q(0, 1)
    tile(0, 1, 0, 256)
    pass_first(qmsg)
    pass_first(kmsg)
    pass_second(qmsg)
    end_near(qmsg)
    prep_q(1, 3)
    sweep(1, 1, 3, 0, 256)
    pass_second(kmsg)
    pass_both(qmsg)
    end_near(kmsg)
    prep_k(1, 3)
    sweep(0, 2, 2, 1, 768)
    pass_both(kmsg)
    end_far(qmsg)
    prep_q(4, 4)
    sweep(4, 2, 2, 0, 1024)
    end_far(kmsg)
    prep_k(4, 4)
    for first in (6, 4, 2, 0):
        tile(first, 2, 4, 1024)
        leave(first + 1)
        leave(first)
    for t in range(3):
        a, b, c = names(t)
        merge(t, 1, a | b)
        back[t, 2, a].start()
        merge(t, 1, b)
        back[t, 2, 0].start()
    for t in range(3):
        a, b, c = names(t)
        merge(t, 1, a)
        merge(t, 2, a)
        back[t, 3, 0].start()
    for t in range(3):
        merge(t, 1, 0)
        merge(t, 2, 0)
    for t in range(3):
        merge(t, 3, 0)

    inv = [1.0 / ac[0, s + 1:s + 2, :] for s in STAT]
    rt = [ac[0, s + 2:s + 3, :] for s in STAT]
    att = jnp.concatenate([ac[0, 0:88, :] * inv[0], ac[0, 96:136, :] * inv[1]], axis=0)
    tan = jnp.concatenate([
        (ac[0, 136:184, :] - att[0:48] * rt[1]) * inv[1],
        (ac[0, 192:272, :] - att[48:128] * rt[2]) * inv[2],
    ], axis=0)
    fin[0] = jnp.transpose(att)
    fin[1] = jnp.transpose(tan)
    away = pl.ds(pl.multiple_of((1 - core) * 128, 128), 128)
    ends = []
    for i, out in enumerate((o, ot)):
        ends.append(pltpu.make_async_remote_copy(
            src_ref=fin.at[i, away], dst_ref=out.at[:, mine],
            send_sem=f_s.at[i], recv_sem=f_r.at[i], device_id=sib, device_id_type=MESH))
        ends.append(pltpu.make_async_copy(fin.at[i, rows], out.at[:, mine], f_o.at[i]))
    for c in ends:
        c.start()
    for c in ends:
        c.wait()
    for c in swaps:
        c.wait_send()
    for m in (kmsg, qmsg, back):
        for c in m.values():
            c.wait_send()


def per_device(queries, keys, values, query_tangent, key_tangent, value_tangent):
    hbm = pl.BlockSpec(memory_space=pl.ANY)
    dma = pltpu.SemaphoreType.DMA
    shape = jax.ShapeDtypeStruct(queries.shape, F32)
    return pl.pallas_call(
        kernel,
        out_shape=(shape, shape),
        in_specs=[hbm] * 6,
        out_specs=(hbm, hbm),
        scratch_shapes=[
            pltpu.VMEM((4, 8, LN, DH), F32),
            pltpu.VMEM((2, 8, LN, DH), F32),
            pltpu.VMEM((2048, 768), BF),
            pltpu.VMEM((2048, 768), BF),
            pltpu.VMEM((256, 2048), BF),
            pltpu.VMEM((256, 2048), BF),
            pltpu.VMEM((2048, 768), BF),
            pltpu.VMEM((2048, 768), BF),
            pltpu.VMEM((8, 280, LN), F32),
            pltpu.VMEM((3, 7, 96, LN), F32),
            pltpu.VMEM((2, LN, DH), F32),
            dma((6,)), dma((6,)), dma((6,)),
            dma((24,)), dma((24,)), dma((24,)), dma((24,)),
            dma((21,)), dma((21,)),
            dma((2,)), dma((2,)), dma((2,)),
        ],
        compiler_params=pltpu.CompilerParams(
            collective_id=0, has_side_effects=True, vmem_limit_bytes=62 << 20
        ),
        name="attention_tangent",
    )(queries, query_tangent, keys, key_tangent, values, value_tangent)


def solution(mesh):
    spec = P(("pb", "kv"), None)
    return jax.shard_map(
        per_device, mesh=mesh, in_specs=(spec,) * 6, out_specs=(spec, spec), check_vma=False
    )
```

```python
import math

import jax
import jax.numpy as jnp
from jax import lax
from jax.experimental import pallas as pl
from jax.experimental.pallas import tpu as pltpu
from jax.sharding import PartitionSpec as P

DH = 128
LN = 128
F32, BF = jnp.float32, jnp.bfloat16
MESH = pl.DeviceIdType.MESH
ORDER = (0, 1, 2, 4, 3, 5, 6, 7)
POS = tuple(ORDER.index(r) for r in range(8))
THIRD = (((0, 48), (48, 40), (88, 40)), ((0, 40), (40, 48), (88, 40)))
PART = ((0, 96), (96, 96), (192, 88))
STAT = (88, 184, 272)


def nt(a, b):
    return lax.dot_general(a, b, (((1,), (1,)), ((), ())), preferred_element_type=F32)


def nn(a, b):
    return jnp.dot(a, b, preferred_element_type=F32)


def two(x):
    hi = x.astype(BF)
    return hi, (x - hi.astype(F32)).astype(BF)


def three(x):
    hi = x.astype(BF)
    rest = x - hi.astype(F32)
    mid = rest.astype(BF)
    return hi, mid, (rest - mid.astype(F32)).astype(BF)


def kernel(q, dq, k, dk, v, dv, o, ot, kvb, qb, ks, ky, vh, vl, qs, qx, ac, rb, fin,
           swap_s, swap_r, own_s, k_s, k_r, q_s, q_r, s_s, s_r, b_s, b_r, f_s, f_r, f_o):
    pb, kv = lax.axis_index("pb"), lax.axis_index("kv")
    core, x = pb % 2, pb // 4
    z, y = (kv // 4) * 2 + (pb // 2) % 2, kv % 4
    head = ((z + 1) // 2) % 2

    def dev(x, y, z, c):
        return (x * 4 + (z % 2) * 2 + c, (z // 2) * 4 + y)

    def near(i):
        return i + 1 - 2 * (i % 2)

    def far(i):
        return (i + 2 * (i % 2) + 3) % 4

    kn = (dev(near(x), y, z, core), dev(x, near(y), z, core))
    qn = (dev(far(x), y, z, core), dev(x, far(y), z, core), dev(x, y, far(z), core))
    mate = dev(x, y, near(z), core)
    sib = dev(x, y, z, 1 - core)

    barrier = pltpu.get_barrier_semaphore()
    for other in kn + qn + (mate, sib):
        pl.semaphore_signal(barrier, inc=1, device_id=other, device_id_type=MESH)
    mine = pl.ds(pl.multiple_of(head * DH, DH), DH)
    theirs = pl.ds(pl.multiple_of((1 - head) * DH, DH), DH)
    table = ((q, qb, 0), (dq, qb, 1), (k, kvb, 0), (dk, kvb, 1), (v, kvb, 2), (dv, kvb, 3))

    def place(dst, a, wave):
        return dst.at[a, 8 * wave] if dst is qb else dst.at[a, 4 * wave, 0]

    owns = [pltpu.make_async_copy(ref.at[:, mine], place(dst, a, 0), own_s.at[i])
            for i, (ref, dst, a) in enumerate(table)]
    for c in owns:
        c.start()
    pl.semaphore_wait(barrier, 7)
    swaps = [pltpu.make_async_remote_copy(
        src_ref=ref.at[:, theirs], dst_ref=place(dst, a, 1), send_sem=swap_s.at[i],
        recv_sem=swap_r.at[i], device_id=mate, device_id_type=MESH)
        for i, (ref, dst, a) in enumerate(table)]
    for c in swaps:
        c.start()

    def names(t):
        return 1 << t, 1 << (t + 1) % 3, 1 << (t + 2) % 3

    def qroute(w, t, to):
        d = [i for i in ((t + j) % 3 for j in range(3)) if to >> i & 1][-1]
        part = pl.ds(*THIRD[w][t])
        i = w * 24 + t * 8 + to
        return pltpu.make_async_remote_copy(
            src_ref=qb.at[:, 8 * w + POS[to ^ (1 << d)], part],
            dst_ref=qb.at[:, 8 * w + POS[to], part],
            send_sem=q_s.at[i], recv_sem=q_r.at[i], device_id=qn[d], device_id_type=MESH)

    qmsg = [{(t, to): qroute(w, t, to) for t in range(3) for to in range(1, 8)} for w in range(2)]

    def begin(m):
        for step in range(3):
            for t in range(3):
                m[t, names(t)[step]].start()

    def pass_first(m):
        for t in range(3):
            a, b, c = names(t)
            m[t, a].wait_recv()
            m[t, a | b].start()
            m[t, a | c].start()

    def pass_second(m):
        for t in range(3):
            a, b, c = names(t)
            m[t, b].wait_recv()
            m[t, b | c].start()

    def pass_both(m):
        for t in range(3):
            a, b, c = names(t)
            m[t, a | b].wait_recv()
            m[t, a | b | c].start()

    def end_near(m):
        for t in range(3):
            m[t, names(t)[2]].wait_recv()

    def end_far(m):
        for t in range(3):
            a, b, c = names(t)
            for to in (a | c, b | c, a | b | c):
                m[t, to].wait_recv()

    def kroute(w, t, to):
        d = 1 - t if to >> (1 - t) & 1 else t
        part = pl.ds(64 * t, 64)
        i = w * 8 + t * 4 + to
        return pltpu.make_async_remote_copy(
            src_ref=kvb.at[:, 4 * w + (to ^ (1 << d)), 0, part],
            dst_ref=kvb.at[:, 4 * w + to, 0, part],
            send_sem=k_s.at[i], recv_sem=k_r.at[i], device_id=kn[d], device_id_type=MESH)

    kmsg = [{(t, to): kroute(w, t, to) for t in range(2) for to in range(1, 4)} for w in range(2)]
    smsg = [pltpu.make_async_remote_copy(
        src_ref=kvb.at[:, i, 0], dst_ref=kvb.at[:, i, 1], send_sem=s_s.at[i],
        recv_sem=s_r.at[i], device_id=sib, device_id_type=MESH) for i in range(8)]

    def kbegin(w):
        for t in range(2):
            kmsg[w][t, 1 << t].start()
        for t in range(2):
            kmsg[w][t, 2 >> t].start()
        smsg[4 * w].start()

    def kpass(w):
        for t in range(2):
            kmsg[w][t, 1 << t].wait_recv()
            kmsg[w][t, 3].start()

    def knear(w):
        for t in range(2):
            kmsg[w][t, 2 >> t].wait_recv()
        smsg[4 * w + 1].start()
        smsg[4 * w + 2].start()

    def kfar(w):
        for t in range(2):
            kmsg[w][t, 3].wait_recv()
        smsg[4 * w + 3].start()

    root = 1.0 / math.sqrt(DH)
    base2 = root * math.log2(math.e)

    def prep_k(first, count):
        for i in range(first, first + count):
            smsg[i].wait_recv()

        def one(i, _):
            r = pl.ds(pl.multiple_of(i * 256, 256), 256)
            kh, km, kl = three(kvb[0, i].reshape(256, DH))
            dh, dm = two(kvb[1, i].reshape(256, DH))
            ks[r, :] = jnp.concatenate([kh, km, kh, km, kl, kh], axis=1)
            ky[r, :] = jnp.concatenate([kh, dh, km, dm, kh, dh], axis=1)
            for a in range(2):
                hi, lo = two(jnp.transpose(kvb[2 + a, i].reshape(256, DH)))
                vh[a * DH:(a + 1) * DH, r] = hi
                vl[a * DH:(a + 1) * DH, r] = lo
            return 0
        lax.fori_loop(first, first + count, one, 0)

    def prep_q(first, count):
        def one(i, _):
            r = pl.ds(pl.multiple_of(i * LN, LN), LN)
            raw = qb[0, i]
            h, m, l = three(raw * base2)
            qs[r, :] = jnp.concatenate([h, h, m, m, h, l], axis=1)
            h, m = two(raw * root)
            dh, dm = two(qb[1, i] * root)
            qx[r, :] = jnp.concatenate([dh, h, dh, h, dm, m], axis=1)
            ac[i] = jnp.zeros(ac.shape[1:], F32)
            ac[i, 88:89, :] = jnp.full((1, LN), -1e30, F32)
            return 0
        lax.fori_loop(first, first + count, one, 0)

    def tile(at, k0, keys):
        first = at * 4
        r = pl.ds(pl.multiple_of(first * LN, 4 * LN), 4 * LN)
        c = slice(k0 * 256, (k0 + keys) * 256)

        def lanes(row):
            return jnp.concatenate([ac[first + i, row:row + 1, :] for i in range(4)], axis=1)

        s = nt(ks[c, :], qs[r, :])
        t = nt(ky[c, :], qx[r, :])
        old = lanes(88)
        peak = jnp.maximum(old, jnp.max(s, axis=0, keepdims=True))
        fade = jnp.exp2(old - peak)
        e = jnp.exp2(s - peak)
        w = e * t
        total = lanes(89) * fade + jnp.sum(e, axis=0, keepdims=True)
        total_t = lanes(90) * fade + jnp.sum(w, axis=0, keepdims=True)
        eh, el = two(e)
        wh, wl = two(w)
        hi, lo = vh[:, c], vl[:, c]
        n = nn(hi, eh) + nn(lo, eh) + nn(hi, el)
        u = nn(hi[:DH], wh) + nn(lo[:DH], wh) + nn(hi[:DH], wl)
        tan = n[DH:] + u
        for i in range(4):
            s_ = slice(i * LN, (i + 1) * LN)
            f = fade[:, s_]
            p = first + i
            ac[p, 0:88, :] = ac[p, 0:88, :] * f + n[0:88, s_]
            ac[p, 96:136, :] = ac[p, 96:136, :] * f + n[88:128, s_]
            ac[p, 136:184, :] = ac[p, 136:184, :] * f + tan[0:48, s_]
            ac[p, 192:272, :] = ac[p, 192:272, :] * f + tan[48:128, s_]
            ac[p, 88:89, :] = peak[:, s_]
            ac[p, 89:90, :] = total[:, s_]
            ac[p, 90:91, :] = total_t[:, s_]

    def sweep(first, count, k0, keys):
        def one(i, _):
            tile(first + i, k0, keys)
            return 0
        lax.fori_loop(0, count, one, 0)

    def bmsg(w, t, src, d, i):
        r0, n = PART[t]
        j = w * 21 + t * 7 + i
        return pltpu.make_async_remote_copy(
            src_ref=ac.at[8 * w + POS[src], pl.ds(r0, n)], dst_ref=rb.at[w, t, i, pl.ds(0, n)],
            send_sem=b_s.at[j], recv_sem=b_r.at[j], device_id=qn[d], device_id_type=MESH)

    back = {}
    for w in range(2):
        for t in range(3):
            a, b, c = names(t)
            for i, to in enumerate((0, a, b, a | b)):
                back[w, t, 1, to] = bmsg(w, t, to | c, (t + 2) % 3, i)
            for i, to in enumerate((0, a)):
                back[w, t, 2, to] = bmsg(w, t, to | b, (t + 1) % 3, 4 + i)
            back[w, t, 3, 0] = bmsg(w, t, a, t, 6)

    def leave(at):
        for p in range(at * 4 + 3, at * 4 - 1, -1):
            ac[p, 184:192, :] = ac[p, 88:96, :]
            ac[p, 272:280, :] = ac[p, 88:96, :]
            w, r = p // 8, ORDER[p % 8]
            for t in range(3):
                c = names(t)[2]
                if r & c:
                    back[w, t, 1, r ^ c].start()

    def merge(w, t, step, to):
        back[w, t, step, to].wait_recv()
        a, b, _ = names(t)
        i = {1: {0: 0, a: 1, b: 2, a | b: 3}, 2: {0: 4, a: 5}, 3: {0: 6}}[step][to]
        r0, n = PART[t]
        st, p = STAT[t], 8 * w + POS[to]
        m1, m2 = ac[p, st:st + 1, :], rb[w, t, i, n - 8:n - 7, :]
        top = jnp.maximum(m1, m2)
        f1, f2 = jnp.exp2(m1 - top), jnp.exp2(m2 - top)
        ac[p, r0:r0 + n, :] = ac[p, r0:r0 + n, :] * f1 + rb[w, t, i, :n, :] * f2
        ac[p, st:st + 1, :] = top

    def back_one(w):
        for t in range(3):
            a, b, c = names(t)
            merge(w, t, 1, a | b)
            back[w, t, 2, a].start()
            merge(w, t, 1, b)
            back[w, t, 2, 0].start()

    def back_two(w):
        for t in range(3):
            a, b, c = names(t)
            merge(w, t, 1, a)
            merge(w, t, 2, a)
            back[w, t, 3, 0].start()

    def back_three(w):
        for t in range(3):
            merge(w, t, 1, 0)
            merge(w, t, 2, 0)
        for t in range(3):
            merge(w, t, 3, 0)
        p = 8 * w
        inv = [1.0 / ac[p, s + 1:s + 2, :] for s in STAT]
        rt = [ac[p, s + 2:s + 3, :] for s in STAT]
        att = jnp.concatenate([ac[p, 0:88, :] * inv[0], ac[p, 96:136, :] * inv[1]], axis=0)
        tan = jnp.concatenate([
            (ac[p, 136:184, :] - att[0:48] * rt[1]) * inv[1],
            (ac[p, 192:272, :] - att[48:128] * rt[2]) * inv[2],
        ], axis=0)
        fin[w, 0] = jnp.transpose(att)
        fin[w, 1] = jnp.transpose(tan)

    outs = [pltpu.make_async_copy(fin.at[0, i], out.at[:, mine], f_o.at[i])
            for i, out in enumerate((o, ot))]
    gifts = [pltpu.make_async_remote_copy(
        src_ref=fin.at[1, i], dst_ref=out.at[:, mine], send_sem=f_s.at[i],
        recv_sem=f_r.at[i], device_id=mate, device_id_type=MESH)
        for i, out in enumerate((o, ot))]

    for c in owns:
        c.wait()
    begin(qmsg[0])
    kbegin(0)
    prep_q(0, 1)
    pass_first(qmsg[0])
    prep_k(0, 1)
    for i in range(2):
        swaps[i].wait_recv()
    begin(qmsg[1])
    pass_second(qmsg[0])
    kpass(0)
    end_near(qmsg[0])
    prep_q(1, 3)
    tile(0, 0, 1)
    pass_both(qmsg[0])
    pass_first(qmsg[1])
    knear(0)
    pass_second(qmsg[1])
    end_far(qmsg[0])
    prep_q(4, 4)
    for i in range(2, 6):
        swaps[i].wait_recv()
    kbegin(1)
    prep_k(1, 2)
    tile(0, 1, 2)
    kfar(0)
    tile(1, 0, 3)
    pass_both(qmsg[1])
    kpass(1)
    prep_k(3, 2)
    sweep(0, 2, 3, 2)
    end_near(qmsg[1])
    end_far(qmsg[1])
    prep_q(8, 8)
    knear(1)
    tile(2, 0, 5)
    kfar(1)
    tile(3, 0, 5)
    prep_k(5, 3)
    tile(3, 5, 3)
    leave(3)
    tile(2, 5, 3)
    leave(2)
    tile(1, 5, 3)
    leave(1)
    back_one(1)
    tile(0, 5, 3)
    leave(0)
    back_two(1)
    back_one(0)
    back_three(1)
    for c in gifts:
        c.start()
    back_two(0)
    back_three(0)
    for c in outs:
        c.start()
    for c in outs + gifts:
        c.wait()
    for c in swaps + smsg:
        c.wait_send()
    for m in kmsg + qmsg + [back]:
        for c in m.values():
            c.wait_send()


def per_device(queries, keys, values, query_tangent, key_tangent, value_tangent):
    hbm = pl.BlockSpec(memory_space=pl.ANY)
    dma = pltpu.SemaphoreType.DMA
    shape = jax.ShapeDtypeStruct(queries.shape, F32)
    return pl.pallas_call(
        kernel,
        out_shape=(shape, shape),
        in_specs=[hbm] * 6,
        out_specs=(hbm, hbm),
        scratch_shapes=[
            pltpu.VMEM((4, 8, 2, LN, DH), F32),
            pltpu.VMEM((2, 16, LN, DH), F32),
            pltpu.VMEM((2048, 768), BF),
            pltpu.VMEM((2048, 768), BF),
            pltpu.VMEM((256, 2048), BF),
            pltpu.VMEM((256, 2048), BF),
            pltpu.VMEM((2048, 768), BF),
            pltpu.VMEM((2048, 768), BF),
            pltpu.VMEM((16, 280, LN), F32),
            pltpu.VMEM((2, 3, 7, 96, LN), F32),
            pltpu.VMEM((2, 2, LN, DH), F32),
            dma((6,)), dma((6,)), dma((6,)),
            dma((16,)), dma((16,)), dma((48,)), dma((48,)),
            dma((8,)), dma((8,)), dma((42,)), dma((42,)),
            dma((2,)), dma((2,)), dma((2,)),
        ],
        compiler_params=pltpu.CompilerParams(
            collective_id=0, has_side_effects=True, vmem_limit_bytes=62 << 20
        ),
        name="attention_tangent",
    )(queries, query_tangent, keys, key_tangent, values, value_tangent)


def solution(mesh):
    spec = P(("pb", "kv"), None)
    return jax.shard_map(
        per_device, mesh=mesh, in_specs=(spec,) * 6, out_specs=(spec, spec), check_vma=False
    )
```

```python
import math

import jax
import jax.numpy as jnp
from jax import lax
from jax.experimental import pallas as pl
from jax.experimental.pallas import tpu as pltpu
from jax.sharding import PartitionSpec as P

DH = 128
LN = 128
F32, BF = jnp.float32, jnp.bfloat16
MESH = pl.DeviceIdType.MESH
ORDER = (0, 1, 2, 4, 3, 5, 6, 7)
POS = tuple(ORDER.index(r) for r in range(8))
THIRD = (((0, 48), (48, 40), (88, 40)), ((0, 40), (40, 48), (88, 40)))
PART = ((0, 96), (96, 96), (192, 88))
STAT = (88, 184, 272)


def nt(a, b):
    return lax.dot_general(a, b, (((1,), (1,)), ((), ())), preferred_element_type=F32)


def nn(a, b):
    return jnp.dot(a, b, preferred_element_type=F32)


def two(x):
    hi = x.astype(BF)
    return hi, (x - hi.astype(F32)).astype(BF)


def three(x):
    hi = x.astype(BF)
    rest = x - hi.astype(F32)
    mid = rest.astype(BF)
    return hi, mid, (rest - mid.astype(F32)).astype(BF)


def kernel(q, dq, k, dk, v, dv, o, ot, kvb, qb, ks, ky, vh, vl, qs, qx, ac, rb, fin,
           swap_s, swap_r, own_s, k_s, k_r, q_s, q_r, s_s, s_r, b_s, b_r, f_s, f_r, f_o):
    pb, kv = lax.axis_index("pb"), lax.axis_index("kv")
    core, x = pb % 2, pb // 4
    z, y = (kv // 4) * 2 + (pb // 2) % 2, kv % 4
    head = ((z + 1) // 2) % 2

    def dev(x, y, z, c):
        return (x * 4 + (z % 2) * 2 + c, (z // 2) * 4 + y)

    def near(i):
        return i + 1 - 2 * (i % 2)

    def far(i):
        return (i + 2 * (i % 2) + 3) % 4

    kn = (dev(near(x), y, z, core), dev(x, near(y), z, core))
    qn = (dev(far(x), y, z, core), dev(x, far(y), z, core), dev(x, y, far(z), core))
    mate = dev(x, y, near(z), core)
    sib = dev(x, y, z, 1 - core)

    barrier = pltpu.get_barrier_semaphore()
    for other in kn + qn + (mate, sib):
        pl.semaphore_signal(barrier, inc=1, device_id=other, device_id_type=MESH)
    mine = pl.ds(pl.multiple_of(head * DH, DH), DH)
    theirs = pl.ds(pl.multiple_of((1 - head) * DH, DH), DH)
    table = ((q, qb, 0), (dq, qb, 1), (k, kvb, 0), (dk, kvb, 1), (v, kvb, 2), (dv, kvb, 3))

    def place(dst, a, wave):
        return dst.at[a, 8 * wave] if dst is qb else dst.at[a, 4 * wave, 0]

    owns = [pltpu.make_async_copy(ref.at[:, mine], place(dst, a, 0), own_s.at[i])
            for i, (ref, dst, a) in enumerate(table)]
    for c in owns:
        c.start()
    pl.semaphore_wait(barrier, 7)
    swaps = [pltpu.make_async_remote_copy(
        src_ref=ref.at[:, theirs], dst_ref=place(dst, a, 1), send_sem=swap_s.at[i],
        recv_sem=swap_r.at[i], device_id=mate, device_id_type=MESH)
        for i, (ref, dst, a) in enumerate(table)]
    for c in swaps:
        c.start()

    def names(t):
        return 1 << t, 1 << (t + 1) % 3, 1 << (t + 2) % 3

    def qroute(w, t, to):
        d = [i for i in ((t + j) % 3 for j in range(3)) if to >> i & 1][-1]
        part = pl.ds(*THIRD[w][t])
        i = w * 24 + t * 8 + to
        return pltpu.make_async_remote_copy(
            src_ref=qb.at[:, 8 * w + POS[to ^ (1 << d)], part],
            dst_ref=qb.at[:, 8 * w + POS[to], part],
            send_sem=q_s.at[i], recv_sem=q_r.at[i], device_id=qn[d], device_id_type=MESH)

    qmsg = [{(t, to): qroute(w, t, to) for t in range(3) for to in range(1, 8)} for w in range(2)]

    def begin(m):
        for step in range(3):
            for t in range(3):
                m[t, names(t)[step]].start()

    def pass_first(m):
        for t in range(3):
            a, b, c = names(t)
            m[t, a].wait_recv()
            m[t, a | b].start()
            m[t, a | c].start()

    def pass_second(m):
        for t in range(3):
            a, b, c = names(t)
            m[t, b].wait_recv()
            m[t, b | c].start()

    def pass_both(m):
        for t in range(3):
            a, b, c = names(t)
            m[t, a | b].wait_recv()
            m[t, a | b | c].start()

    def end_near(m):
        for t in range(3):
            m[t, names(t)[2]].wait_recv()

    def end_far(m):
        for t in range(3):
            a, b, c = names(t)
            for to in (a | c, b | c, a | b | c):
                m[t, to].wait_recv()

    def kroute(w, t, to):
        d = 1 - t if to >> (1 - t) & 1 else t
        part = pl.ds(64 * t, 64)
        i = w * 8 + t * 4 + to
        return pltpu.make_async_remote_copy(
            src_ref=kvb.at[:, 4 * w + (to ^ (1 << d)), 0, part],
            dst_ref=kvb.at[:, 4 * w + to, 0, part],
            send_sem=k_s.at[i], recv_sem=k_r.at[i], device_id=kn[d], device_id_type=MESH)

    kmsg = [{(t, to): kroute(w, t, to) for t in range(2) for to in range(1, 4)} for w in range(2)]
    smsg = [pltpu.make_async_remote_copy(
        src_ref=kvb.at[:, i, 0], dst_ref=kvb.at[:, i, 1], send_sem=s_s.at[i],
        recv_sem=s_r.at[i], device_id=sib, device_id_type=MESH) for i in range(8)]

    def kbegin(w):
        for t in range(2):
            kmsg[w][t, 1 << t].start()
        for t in range(2):
            kmsg[w][t, 2 >> t].start()
        smsg[4 * w].start()

    def kpass(w):
        for t in range(2):
            kmsg[w][t, 1 << t].wait_recv()
            kmsg[w][t, 3].start()

    def knear(w):
        for t in range(2):
            kmsg[w][t, 2 >> t].wait_recv()
        smsg[4 * w + 1].start()
        smsg[4 * w + 2].start()

    def kfar(w):
        for t in range(2):
            kmsg[w][t, 3].wait_recv()
        smsg[4 * w + 3].start()

    root = 1.0 / math.sqrt(DH)
    base2 = root * math.log2(math.e)

    def prep_k(first, count):
        for i in range(first, first + count):
            smsg[i].wait_recv()

        def one(i, _):
            r = pl.ds(pl.multiple_of(i * 256, 256), 256)
            kh, km, kl = three(kvb[0, i].reshape(256, DH))
            dh, dm = two(kvb[1, i].reshape(256, DH))
            ks[r, :] = jnp.concatenate([kh, km, kh, km, kl, kh], axis=1)
            ky[r, :] = jnp.concatenate([kh, dh, km, dm, kh, dh], axis=1)
            for a in range(2):
                hi, lo = two(jnp.transpose(kvb[2 + a, i].reshape(256, DH)))
                vh[a * DH:(a + 1) * DH, r] = hi
                vl[a * DH:(a + 1) * DH, r] = lo
            return 0
        lax.fori_loop(first, first + count, one, 0)

    def prep_q(first, count):
        def one(i, _):
            r = pl.ds(pl.multiple_of(i * LN, LN), LN)
            raw = qb[0, i]
            h, m, l = three(raw * base2)
            qs[r, :] = jnp.concatenate([h, h, m, m, h, l], axis=1)
            h, m = two(raw * root)
            dh, dm = two(qb[1, i] * root)
            qx[r, :] = jnp.concatenate([dh, h, dh, h, dm, m], axis=1)
            ac[i] = jnp.zeros(ac.shape[1:], F32)
            ac[i, 88:89, :] = jnp.full((1, LN), -1e30, F32)
            return 0
        lax.fori_loop(first, first + count, one, 0)

    def tile(at, k0, keys):
        first = at * 4
        r = pl.ds(pl.multiple_of(first * LN, 4 * LN), 4 * LN)
        c = slice(k0 * 256, (k0 + keys) * 256)

        def lanes(row):
            return jnp.concatenate([ac[first + i, row:row + 1, :] for i in range(4)], axis=1)

        s = nt(ks[c, :], qs[r, :])
        t = nt(ky[c, :], qx[r, :])
        old = lanes(88)
        peak = jnp.maximum(old, jnp.max(s, axis=0, keepdims=True))
        fade = jnp.exp2(old - peak)
        e = jnp.exp2(s - peak)
        w = e * t
        total = lanes(89) * fade + jnp.sum(e, axis=0, keepdims=True)
        total_t = lanes(90) * fade + jnp.sum(w, axis=0, keepdims=True)
        eh, el = two(e)
        wh, wl = two(w)
        hi, lo = vh[:, c], vl[:, c]
        n = nn(hi, eh) + nn(lo, eh) + nn(hi, el)
        u = nn(hi[:DH], wh) + nn(lo[:DH], wh) + nn(hi[:DH], wl)
        tan = n[DH:] + u
        for i in range(4):
            s_ = slice(i * LN, (i + 1) * LN)
            f = fade[:, s_]
            p = first + i
            ac[p, 0:88, :] = ac[p, 0:88, :] * f + n[0:88, s_]
            ac[p, 96:136, :] = ac[p, 96:136, :] * f + n[88:128, s_]
            ac[p, 136:184, :] = ac[p, 136:184, :] * f + tan[0:48, s_]
            ac[p, 192:272, :] = ac[p, 192:272, :] * f + tan[48:128, s_]
            ac[p, 88:89, :] = peak[:, s_]
            ac[p, 89:90, :] = total[:, s_]
            ac[p, 90:91, :] = total_t[:, s_]

    def sweep(first, count, k0, keys):
        def one(i, _):
            tile(first + i, k0, keys)
            return 0
        lax.fori_loop(0, count, one, 0)

    def bmsg(w, t, src, d, i):
        r0, n = PART[t]
        j = w * 21 + t * 7 + i
        return pltpu.make_async_remote_copy(
            src_ref=ac.at[8 * w + POS[src], pl.ds(r0, n)], dst_ref=rb.at[w, t, i, pl.ds(0, n)],
            send_sem=b_s.at[j], recv_sem=b_r.at[j], device_id=qn[d], device_id_type=MESH)

    back = {}
    for w in range(2):
        for t in range(3):
            a, b, c = names(t)
            for i, to in enumerate((0, a, b, a | b)):
                back[w, t, 1, to] = bmsg(w, t, to | c, (t + 2) % 3, i)
            for i, to in enumerate((0, a)):
                back[w, t, 2, to] = bmsg(w, t, to | b, (t + 1) % 3, 4 + i)
            back[w, t, 3, 0] = bmsg(w, t, a, t, 6)

    def leave(at):
        for p in range(at * 4 + 3, at * 4 - 1, -1):
            ac[p, 184:192, :] = ac[p, 88:96, :]
            ac[p, 272:280, :] = ac[p, 88:96, :]
            w, r = p // 8, ORDER[p % 8]
            for t in range(3):
                c = names(t)[2]
                if r & c:
                    back[w, t, 1, r ^ c].start()

    def merge(w, t, step, to):
        back[w, t, step, to].wait_recv()
        a, b, _ = names(t)
        i = {1: {0: 0, a: 1, b: 2, a | b: 3}, 2: {0: 4, a: 5}, 3: {0: 6}}[step][to]
        r0, n = PART[t]
        st, p = STAT[t], 8 * w + POS[to]
        m1, m2 = ac[p, st:st + 1, :], rb[w, t, i, n - 8:n - 7, :]
        top = jnp.maximum(m1, m2)
        f1, f2 = jnp.exp2(m1 - top), jnp.exp2(m2 - top)
        ac[p, r0:r0 + n, :] = ac[p, r0:r0 + n, :] * f1 + rb[w, t, i, :n, :] * f2
        ac[p, st:st + 1, :] = top

    def back_far(w):
        for t in range(3):
            a, b, c = names(t)
            merge(w, t, 1, a | b)
            back[w, t, 2, a].start()

    def back_near(w):
        for t in range(3):
            a, b, c = names(t)
            merge(w, t, 1, b)
            back[w, t, 2, 0].start()
        for t in range(3):
            a, b, c = names(t)
            merge(w, t, 1, a)
            merge(w, t, 2, a)
            back[w, t, 3, 0].start()

    def back_three(w):
        for t in range(3):
            merge(w, t, 1, 0)
            merge(w, t, 2, 0)
        for t in range(3):
            merge(w, t, 3, 0)
        p = 8 * w
        inv = [1.0 / ac[p, s + 1:s + 2, :] for s in STAT]
        rt = [ac[p, s + 2:s + 3, :] for s in STAT]
        att = jnp.concatenate([ac[p, 0:88, :] * inv[0], ac[p, 96:136, :] * inv[1]], axis=0)
        tan = jnp.concatenate([
            (ac[p, 136:184, :] - att[0:48] * rt[1]) * inv[1],
            (ac[p, 192:272, :] - att[48:128] * rt[2]) * inv[2],
        ], axis=0)
        fin[w, 0] = jnp.transpose(att)
        fin[w, 1] = jnp.transpose(tan)

    outs = [pltpu.make_async_copy(fin.at[0, i], out.at[:, mine], f_o.at[i])
            for i, out in enumerate((o, ot))]
    gifts = [pltpu.make_async_remote_copy(
        src_ref=fin.at[1, i], dst_ref=out.at[:, mine], send_sem=f_s.at[i],
        recv_sem=f_r.at[i], device_id=mate, device_id_type=MESH)
        for i, out in enumerate((o, ot))]

    for c in owns:
        c.wait()
    begin(qmsg[0])
    kbegin(0)
    prep_q(0, 1)
    pass_first(qmsg[0])
    prep_k(0, 1)
    for i in range(2):
        swaps[i].wait_recv()
    begin(qmsg[1])
    pass_second(qmsg[0])
    kpass(0)
    end_near(qmsg[0])
    prep_q(1, 3)
    tile(0, 0, 1)
    pass_both(qmsg[0])
    pass_first(qmsg[1])
    knear(0)
    pass_second(qmsg[1])
    end_far(qmsg[0])
    prep_q(4, 4)
    for i in range(2, 6):
        swaps[i].wait_recv()
    kbegin(1)
    prep_k(1, 2)
    tile(0, 1, 2)
    kfar(0)
    pass_both(qmsg[1])
    tile(1, 0, 3)
    kpass(1)
    prep_k(3, 2)
    sweep(0, 2, 3, 2)
    end_near(qmsg[1])
    end_far(qmsg[1])
    prep_q(8, 8)
    knear(1)
    tile(2, 0, 5)
    kfar(1)
    tile(3, 0, 5)
    prep_k(5, 3)
    tile(3, 5, 3)
    leave(3)
    tile(2, 5, 3)
    leave(2)
    back_far(1)
    tile(1, 5, 3)
    leave(1)
    back_near(1)
    tile(0, 5, 3)
    leave(0)
    back_far(0)
    back_near(0)
    back_three(1)
    for c in gifts:
        c.start()
    back_three(0)
    for c in outs:
        c.start()
    for c in outs + gifts:
        c.wait()
    for c in swaps + smsg:
        c.wait_send()
    for m in kmsg + qmsg + [back]:
        for c in m.values():
            c.wait_send()


def per_device(queries, keys, values, query_tangent, key_tangent, value_tangent):
    hbm = pl.BlockSpec(memory_space=pl.ANY)
    dma = pltpu.SemaphoreType.DMA
    shape = jax.ShapeDtypeStruct(queries.shape, F32)
    return pl.pallas_call(
        kernel,
        out_shape=(shape, shape),
        in_specs=[hbm] * 6,
        out_specs=(hbm, hbm),
        scratch_shapes=[
            pltpu.VMEM((4, 8, 2, LN, DH), F32),
            pltpu.VMEM((2, 16, LN, DH), F32),
            pltpu.VMEM((2048, 768), BF),
            pltpu.VMEM((2048, 768), BF),
            pltpu.VMEM((256, 2048), BF),
            pltpu.VMEM((256, 2048), BF),
            pltpu.VMEM((2048, 768), BF),
            pltpu.VMEM((2048, 768), BF),
            pltpu.VMEM((16, 280, LN), F32),
            pltpu.VMEM((2, 3, 7, 96, LN), F32),
            pltpu.VMEM((2, 2, LN, DH), F32),
            dma((6,)), dma((6,)), dma((6,)),
            dma((16,)), dma((16,)), dma((48,)), dma((48,)),
            dma((8,)), dma((8,)), dma((42,)), dma((42,)),
            dma((2,)), dma((2,)), dma((2,)),
        ],
        compiler_params=pltpu.CompilerParams(
            collective_id=0, has_side_effects=True, vmem_limit_bytes=62 << 20
        ),
        name="attention_tangent",
    )(queries, query_tangent, keys, key_tangent, values, value_tangent)


def solution(mesh):
    spec = P(("pb", "kv"), None)
    return jax.shard_map(
        per_device, mesh=mesh, in_specs=(spec,) * 6, out_specs=(spec, spec), check_vma=False
    )
```

```python
import math

import jax
import jax.numpy as jnp
from jax import lax
from jax.experimental import pallas as pl
from jax.experimental.pallas import tpu as pltpu
from jax.sharding import PartitionSpec as P

DH = 128
LN = 128
F32, BF = jnp.float32, jnp.bfloat16
MESH = pl.DeviceIdType.MESH
ORDER = (0, 1, 2, 4, 3, 5, 6, 7)
POS = tuple(ORDER.index(r) for r in range(8))
THIRD = (((0, 48), (48, 40), (88, 40)), ((0, 40), (40, 48), (88, 40)))
PART = ((0, 96), (96, 96), (192, 88))
STAT = (88, 184, 272)


def nt(a, b):
    return lax.dot_general(a, b, (((1,), (1,)), ((), ())), preferred_element_type=F32)


def nn(a, b):
    return jnp.dot(a, b, preferred_element_type=F32)


def two(x):
    hi = x.astype(BF)
    return hi, (x - hi.astype(F32)).astype(BF)


def three(x):
    hi = x.astype(BF)
    rest = x - hi.astype(F32)
    mid = rest.astype(BF)
    return hi, mid, (rest - mid.astype(F32)).astype(BF)


def kernel(q, dq, k, dk, v, dv, oo, kvb, qb, ks, ky, vh, vl, qs, qx, ac, rb, fin,
           swap_s, swap_r, own_s, k_s, k_r, q_s, q_r, s_s, s_r, b_s, b_r, f_s, f_r, f_o):
    o, ot = oo.at[0], oo.at[1]
    pb, kv = lax.axis_index("pb"), lax.axis_index("kv")
    core, x = pb % 2, pb // 4
    z, y = (kv // 4) * 2 + (pb // 2) % 2, kv % 4
    head = ((z + 1) // 2) % 2

    def dev(x, y, z, c):
        return (x * 4 + (z % 2) * 2 + c, (z // 2) * 4 + y)

    def near(i):
        return i + 1 - 2 * (i % 2)

    def far(i):
        return (i + 2 * (i % 2) + 3) % 4

    kn = (dev(near(x), y, z, core), dev(x, near(y), z, core))
    qn = (dev(far(x), y, z, core), dev(x, far(y), z, core), dev(x, y, far(z), core))
    mate = dev(x, y, near(z), core)
    sib = dev(x, y, z, 1 - core)

    barrier = pltpu.get_barrier_semaphore()
    for other in kn + qn + (mate, sib):
        pl.semaphore_signal(barrier, inc=1, device_id=other, device_id_type=MESH)
    mine = pl.ds(pl.multiple_of(head * DH, DH), DH)
    theirs = pl.ds(pl.multiple_of((1 - head) * DH, DH), DH)
    table = ((q, qb, 0), (dq, qb, 1), (k, kvb, 0), (dk, kvb, 1), (v, kvb, 2), (dv, kvb, 3))

    def place(dst, a, wave):
        return dst.at[a, 8 * wave] if dst is qb else dst.at[a, 4 * wave, 0]

    owns = [pltpu.make_async_copy(ref.at[:, mine], place(dst, a, 0), own_s.at[i])
            for i, (ref, dst, a) in enumerate(table)]
    for c in owns:
        c.start()
    pl.semaphore_wait(barrier, 7)
    swaps = [pltpu.make_async_remote_copy(
        src_ref=ref.at[:, theirs], dst_ref=place(dst, a, 1), send_sem=swap_s.at[i],
        recv_sem=swap_r.at[i], device_id=mate, device_id_type=MESH)
        for i, (ref, dst, a) in enumerate(table)]
    for c in swaps:
        c.start()

    def names(t):
        return 1 << t, 1 << (t + 1) % 3, 1 << (t + 2) % 3

    def qroute(w, t, to):
        d = [i for i in ((t + j) % 3 for j in range(3)) if to >> i & 1][-1]
        part = pl.ds(*THIRD[w][t])
        i = w * 24 + t * 8 + to
        return pltpu.make_async_remote_copy(
            src_ref=qb.at[:, 8 * w + POS[to ^ (1 << d)], part],
            dst_ref=qb.at[:, 8 * w + POS[to], part],
            send_sem=q_s.at[i], recv_sem=q_r.at[i], device_id=qn[d], device_id_type=MESH)

    qmsg = [{(t, to): qroute(w, t, to) for t in range(3) for to in range(1, 8)} for w in range(2)]

    def begin(m):
        for step in range(3):
            for t in range(3):
                m[t, names(t)[step]].start()

    def pass_first(m):
        for t in range(3):
            a, b, c = names(t)
            m[t, a].wait_recv()
            m[t, a | b].start()
            m[t, a | c].start()

    def pass_second(m):
        for t in range(3):
            a, b, c = names(t)
            m[t, b].wait_recv()
            m[t, b | c].start()

    def pass_both(m):
        for t in range(3):
            a, b, c = names(t)
            m[t, a | b].wait_recv()
            m[t, a | b | c].start()

    def end_near(m):
        for t in range(3):
            m[t, names(t)[2]].wait_recv()

    def end_far(m):
        for t in range(3):
            a, b, c = names(t)
            for to in (a | c, b | c, a | b | c):
                m[t, to].wait_recv()

    def kroute(w, t, to):
        d = 1 - t if to >> (1 - t) & 1 else t
        part = pl.ds(64 * t, 64)
        i = w * 8 + t * 4 + to
        return pltpu.make_async_remote_copy(
            src_ref=kvb.at[:, 4 * w + (to ^ (1 << d)), 0, part],
            dst_ref=kvb.at[:, 4 * w + to, 0, part],
            send_sem=k_s.at[i], recv_sem=k_r.at[i], device_id=kn[d], device_id_type=MESH)

    kmsg = [{(t, to): kroute(w, t, to) for t in range(2) for to in range(1, 4)} for w in range(2)]
    smsg = [pltpu.make_async_remote_copy(
        src_ref=kvb.at[:, i, 0], dst_ref=kvb.at[:, i, 1], send_sem=s_s.at[i],
        recv_sem=s_r.at[i], device_id=sib, device_id_type=MESH) for i in range(8)]

    def kbegin(w):
        for t in range(2):
            kmsg[w][t, 1 << t].start()
        for t in range(2):
            kmsg[w][t, 2 >> t].start()
        smsg[4 * w].start()

    def kpass(w):
        for t in range(2):
            kmsg[w][t, 1 << t].wait_recv()
            kmsg[w][t, 3].start()

    def knear(w):
        for t in range(2):
            kmsg[w][t, 2 >> t].wait_recv()
        smsg[4 * w + 1].start()
        smsg[4 * w + 2].start()

    def kfar(w):
        for t in range(2):
            kmsg[w][t, 3].wait_recv()
        smsg[4 * w + 3].start()

    root = 1.0 / math.sqrt(DH)
    base2 = root * math.log2(math.e)

    def prep_k(first, count):
        for i in range(first, first + count):
            smsg[i].wait_recv()

        def one(i, _):
            r = pl.ds(pl.multiple_of(i * 256, 256), 256)
            kh, km, kl = three(kvb[0, i].reshape(256, DH))
            dh, dm = two(kvb[1, i].reshape(256, DH))
            ks[r, :] = jnp.concatenate([kh, km, kh, km, kl, kh], axis=1)
            ky[r, :] = jnp.concatenate([kh, dh, km, dm, kh, dh], axis=1)
            for a in range(2):
                hi, lo = two(jnp.transpose(kvb[2 + a, i].reshape(256, DH)))
                vh[a * DH:(a + 1) * DH, r] = hi
                vl[a * DH:(a + 1) * DH, r] = lo
            return 0
        lax.fori_loop(first, first + count, one, 0)

    def prep_q(first, count):
        def one(i, _):
            r = pl.ds(pl.multiple_of(i * LN, LN), LN)
            raw = qb[0, i]
            h, m, l = three(raw * base2)
            qs[r, :] = jnp.concatenate([h, h, m, m, h, l], axis=1)
            h, m = two(raw * root)
            dh, dm = two(qb[1, i] * root)
            qx[r, :] = jnp.concatenate([dh, h, dh, h, dm, m], axis=1)
            ac[i] = jnp.zeros(ac.shape[1:], F32)
            ac[i, 88:89, :] = jnp.full((1, LN), -1e30, F32)
            return 0
        lax.fori_loop(first, first + count, one, 0)

    def tile(at, k0, keys):
        first = at * 4
        r = pl.ds(pl.multiple_of(first * LN, 4 * LN), 4 * LN)
        c = slice(k0 * 256, (k0 + keys) * 256)

        def lanes(row):
            return jnp.concatenate([ac[first + i, row:row + 1, :] for i in range(4)], axis=1)

        s = nt(ks[c, :], qs[r, :])
        t = nt(ky[c, :], qx[r, :])
        old = lanes(88)
        peak = jnp.maximum(old, jnp.max(s, axis=0, keepdims=True))
        fade = jnp.exp2(old - peak)
        e = jnp.exp2(s - peak)
        w = e * t
        total = lanes(89) * fade + jnp.sum(e, axis=0, keepdims=True)
        total_t = lanes(90) * fade + jnp.sum(w, axis=0, keepdims=True)
        eh, el = two(e)
        wh, wl = two(w)
        hi, lo = vh[:, c], vl[:, c]
        n = nn(hi, eh) + nn(lo, eh) + nn(hi, el)
        u = nn(hi[:DH], wh) + nn(lo[:DH], wh) + nn(hi[:DH], wl)
        tan = n[DH:] + u
        for i in range(4):
            s_ = slice(i * LN, (i + 1) * LN)
            f = fade[:, s_]
            p = first + i
            ac[p, 0:88, :] = ac[p, 0:88, :] * f + n[0:88, s_]
            ac[p, 96:136, :] = ac[p, 96:136, :] * f + n[88:128, s_]
            ac[p, 136:184, :] = ac[p, 136:184, :] * f + tan[0:48, s_]
            ac[p, 192:272, :] = ac[p, 192:272, :] * f + tan[48:128, s_]
            ac[p, 88:89, :] = peak[:, s_]
            ac[p, 89:90, :] = total[:, s_]
            ac[p, 90:91, :] = total_t[:, s_]

    def sweep(first, count, k0, keys):
        def one(i, _):
            tile(first + i, k0, keys)
            return 0
        lax.fori_loop(0, count, one, 0)

    def bmsg(w, t, src, d, i):
        r0, n = PART[t]
        j = w * 21 + t * 7 + i
        return pltpu.make_async_remote_copy(
            src_ref=ac.at[8 * w + POS[src], pl.ds(r0, n)], dst_ref=rb.at[w, t, i, pl.ds(0, n)],
            send_sem=b_s.at[j], recv_sem=b_r.at[j], device_id=qn[d], device_id_type=MESH)

    back = {}
    for w in range(2):
        for t in range(3):
            a, b, c = names(t)
            for i, to in enumerate((0, a, b, a | b)):
                back[w, t, 1, to] = bmsg(w, t, to | c, (t + 2) % 3, i)
            for i, to in enumerate((0, a)):
                back[w, t, 2, to] = bmsg(w, t, to | b, (t + 1) % 3, 4 + i)
            back[w, t, 3, 0] = bmsg(w, t, a, t, 6)

    def leave(at):
        for p in range(at * 4 + 3, at * 4 - 1, -1):
            ac[p, 184:192, :] = ac[p, 88:96, :]
            ac[p, 272:280, :] = ac[p, 88:96, :]
            w, r = p // 8, ORDER[p % 8]
            for t in range(3):
                c = names(t)[2]
                if r & c:
                    back[w, t, 1, r ^ c].start()

    def merge(w, t, step, to):
        back[w, t, step, to].wait_recv()
        a, b, _ = names(t)
        i = {1: {0: 0, a: 1, b: 2, a | b: 3}, 2: {0: 4, a: 5}, 3: {0: 6}}[step][to]
        r0, n = PART[t]
        st, p = STAT[t], 8 * w + POS[to]
        m1, m2 = ac[p, st:st + 1, :], rb[w, t, i, n - 8:n - 7, :]
        top = jnp.maximum(m1, m2)
        f1, f2 = jnp.exp2(m1 - top), jnp.exp2(m2 - top)
        ac[p, r0:r0 + n, :] = ac[p, r0:r0 + n, :] * f1 + rb[w, t, i, :n, :] * f2
        ac[p, st:st + 1, :] = top

    def back_far(w):
        for t in range(3):
            a, b, c = names(t)
            merge(w, t, 1, a | b)
            back[w, t, 2, a].start()

    def back_near(w):
        for t in range(3):
            a, b, c = names(t)
            merge(w, t, 1, b)
            back[w, t, 2, 0].start()
        for t in range(3):
            a, b, c = names(t)
            merge(w, t, 1, a)
            merge(w, t, 2, a)
            back[w, t, 3, 0].start()

    def back_three(w):
        for t in range(3):
            merge(w, t, 1, 0)
            merge(w, t, 2, 0)
        for t in range(3):
            merge(w, t, 3, 0)
        p = 8 * w
        inv = [1.0 / ac[p, s + 1:s + 2, :] for s in STAT]
        rt = [ac[p, s + 2:s + 3, :] for s in STAT]
        att = jnp.concatenate([ac[p, 0:88, :] * inv[0], ac[p, 96:136, :] * inv[1]], axis=0)
        tan = jnp.concatenate([
            (ac[p, 136:184, :] - att[0:48] * rt[1]) * inv[1],
            (ac[p, 192:272, :] - att[48:128] * rt[2]) * inv[2],
        ], axis=0)
        fin[w, 0] = jnp.transpose(att)
        fin[w, 1] = jnp.transpose(tan)

    outs = [pltpu.make_async_copy(fin.at[0, i], out.at[:, mine], f_o.at[i])
            for i, out in enumerate((o, ot))]
    gifts = [pltpu.make_async_remote_copy(
        src_ref=fin.at[1, i], dst_ref=out.at[:, mine], send_sem=f_s.at[i],
        recv_sem=f_r.at[i], device_id=mate, device_id_type=MESH)
        for i, out in enumerate((o, ot))]

    for c in owns:
        c.wait()
    begin(qmsg[0])
    kbegin(0)
    prep_q(0, 1)
    pass_first(qmsg[0])
    prep_k(0, 1)
    pass_second(qmsg[0])
    kpass(0)
    end_near(qmsg[0])
    prep_q(1, 3)
    pass_both(qmsg[0])
    for i in range(2):
        swaps[i].wait_recv()
    begin(qmsg[1])
    tile(0, 0, 1)
    knear(0)
    for i in range(2, 6):
        swaps[i].wait_recv()
    kbegin(1)
    prep_k(1, 2)
    tile(0, 1, 2)
    pass_first(qmsg[1])
    end_far(qmsg[0])
    prep_q(4, 4)
    kfar(0)
    tile(1, 0, 3)
    pass_second(qmsg[1])
    kpass(1)
    pass_both(qmsg[1])
    prep_k(3, 2)
    sweep(0, 2, 3, 2)
    end_near(qmsg[1])
    prep_q(8, 4)
    tile(2, 0, 5)
    knear(1)
    end_far(qmsg[1])
    prep_q(12, 4)
    tile(3, 0, 5)
    kfar(1)
    prep_k(5, 3)
    tile(3, 5, 3)
    leave(3)
    tile(1, 5, 3)
    leave(1)
    back_far(1)
    tile(2, 5, 3)
    leave(2)
    back_far(0)
    back_near(1)
    tile(0, 5, 3)
    leave(0)
    back_near(0)
    back_three(1)
    for c in gifts:
        c.start()
    back_three(0)
    for c in outs:
        c.start()
    for c in outs + gifts:
        c.wait()
    for c in swaps + smsg:
        c.wait_send()
    for m in kmsg + qmsg + [back]:
        for c in m.values():
            c.wait_send()


def per_device(queries, keys, values, query_tangent, key_tangent, value_tangent):
    hbm = pl.BlockSpec(memory_space=pl.ANY)
    dma = pltpu.SemaphoreType.DMA
    shape = jax.ShapeDtypeStruct((2,) + queries.shape, F32)
    both = pl.pallas_call(
        kernel,
        out_shape=shape,
        in_specs=[hbm] * 6,
        out_specs=hbm,
        scratch_shapes=[
            pltpu.VMEM((4, 8, 2, LN, DH), F32),
            pltpu.VMEM((2, 16, LN, DH), F32),
            pltpu.VMEM((2048, 768), BF),
            pltpu.VMEM((2048, 768), BF),
            pltpu.VMEM((256, 2048), BF),
            pltpu.VMEM((256, 2048), BF),
            pltpu.VMEM((2048, 768), BF),
            pltpu.VMEM((2048, 768), BF),
            pltpu.VMEM((16, 280, LN), F32),
            pltpu.VMEM((2, 3, 7, 96, LN), F32),
            pltpu.VMEM((2, 2, LN, DH), F32),
            dma((6,)), dma((6,)), dma((6,)),
            dma((16,)), dma((16,)), dma((48,)), dma((48,)),
            dma((8,)), dma((8,)), dma((42,)), dma((42,)),
            dma((2,)), dma((2,)), dma((2,)),
        ],
        compiler_params=pltpu.CompilerParams(
            collective_id=0, has_side_effects=True, vmem_limit_bytes=62 << 20
        ),
        name="attention_tangent",
    )(queries, query_tangent, keys, key_tangent, values, value_tangent)
    return both[0], both[1]


def solution(mesh):
    spec = P(("pb", "kv"), None)
    return jax.shard_map(
        per_device, mesh=mesh, in_specs=(spec,) * 6, out_specs=(spec, spec), check_vma=False
    )
```

```python
import math

import jax
import jax.numpy as jnp
from jax import lax
from jax.experimental import pallas as pl
from jax.experimental.pallas import tpu as pltpu
from jax.sharding import PartitionSpec as P

DH = 128
LN = 128
F32, BF = jnp.float32, jnp.bfloat16
MESH = pl.DeviceIdType.MESH
ORDER = (0, 1, 2, 4, 3, 5, 6, 7)
POS = tuple(ORDER.index(r) for r in range(8))
THIRD = (((0, 48), (48, 40), (88, 40)), ((0, 40), (40, 48), (88, 40)))
PART = ((0, 96), (96, 96), (192, 88))
STAT = (88, 184, 272)


def nt(a, b):
    return lax.dot_general(a, b, (((1,), (1,)), ((), ())), preferred_element_type=F32)


def nn(a, b):
    return jnp.dot(a, b, preferred_element_type=F32)


def two(x):
    hi = x.astype(BF)
    return hi, (x - hi.astype(F32)).astype(BF)


def three(x):
    hi = x.astype(BF)
    rest = x - hi.astype(F32)
    mid = rest.astype(BF)
    return hi, mid, (rest - mid.astype(F32)).astype(BF)


def kernel(q, dq, k, dk, v, dv, oo, kvb, qb, ks, ky, vh, vl, qs, qx, ac, rb, fin,
           swap_s, swap_r, own_s, k_s, k_r, q_s, q_r, s_s, s_r, b_s, b_r, f_s, f_r, f_o):
    o, ot = oo.at[0], oo.at[1]
    pb, kv = lax.axis_index("pb"), lax.axis_index("kv")
    core, x = pb % 2, pb // 4
    z, y = (kv // 4) * 2 + (pb // 2) % 2, kv % 4
    head = ((z + 1) // 2) % 2

    def dev(x, y, z, c):
        return (x * 4 + (z % 2) * 2 + c, (z // 2) * 4 + y)

    def near(i):
        return i + 1 - 2 * (i % 2)

    def far(i):
        return (i + 2 * (i % 2) + 3) % 4

    kn = (dev(near(x), y, z, core), dev(x, near(y), z, core))
    qn = (dev(far(x), y, z, core), dev(x, far(y), z, core), dev(x, y, far(z), core))
    mate = dev(x, y, near(z), core)
    sib = dev(x, y, z, 1 - core)

    barrier = pltpu.get_barrier_semaphore()
    for other in kn + qn + (mate, sib):
        pl.semaphore_signal(barrier, inc=1, device_id=other, device_id_type=MESH)
    mine = pl.ds(pl.multiple_of(head * DH, DH), DH)
    theirs = pl.ds(pl.multiple_of((1 - head) * DH, DH), DH)
    table = ((q, qb, 0), (dq, qb, 1), (k, kvb, 0), (dk, kvb, 1), (v, kvb, 2), (dv, kvb, 3))

    def place(dst, a, wave):
        return dst.at[a, 8 * wave] if dst is qb else dst.at[a, 4 * wave, 0]

    owns = [pltpu.make_async_copy(ref.at[:, mine], place(dst, a, 0), own_s.at[i])
            for i, (ref, dst, a) in enumerate(table)]
    for c in owns:
        c.start()
    pl.semaphore_wait(barrier, 7)
    swaps = [pltpu.make_async_remote_copy(
        src_ref=ref.at[:, theirs], dst_ref=place(dst, a, 1), send_sem=swap_s.at[i],
        recv_sem=swap_r.at[i], device_id=mate, device_id_type=MESH)
        for i, (ref, dst, a) in enumerate(table)]
    for c in swaps:
        c.start()

    def names(t):
        return 1 << t, 1 << (t + 1) % 3, 1 << (t + 2) % 3

    def qroute(w, t, to):
        d = [i for i in ((t + j) % 3 for j in range(3)) if to >> i & 1][-1]
        part = pl.ds(*THIRD[w][t])
        i = w * 24 + t * 8 + to
        return pltpu.make_async_remote_copy(
            src_ref=qb.at[:, 8 * w + POS[to ^ (1 << d)], part],
            dst_ref=qb.at[:, 8 * w + POS[to], part],
            send_sem=q_s.at[i], recv_sem=q_r.at[i], device_id=qn[d], device_id_type=MESH)

    qmsg = [{(t, to): qroute(w, t, to) for t in range(3) for to in range(1, 8)} for w in range(2)]

    def begin(m):
        for step in range(3):
            for t in range(3):
                m[t, names(t)[step]].start()

    def pass_first(m):
        for t in range(3):
            a, b, c = names(t)
            m[t, a].wait_recv()
            m[t, a | b].start()
            m[t, a | c].start()

    def pass_second(m):
        for t in range(3):
            a, b, c = names(t)
            m[t, b].wait_recv()
            m[t, b | c].start()

    def pass_both(m):
        for t in range(3):
            a, b, c = names(t)
            m[t, a | b].wait_recv()
            m[t, a | b | c].start()

    def end_near(m):
        for t in range(3):
            m[t, names(t)[2]].wait_recv()

    def end_far(m):
        for t in range(3):
            a, b, c = names(t)
            for to in (a | c, b | c, a | b | c):
                m[t, to].wait_recv()

    def kroute(w, t, to):
        d = 1 - t if to >> (1 - t) & 1 else t
        part = pl.ds(64 * t, 64)
        i = w * 8 + t * 4 + to
        return pltpu.make_async_remote_copy(
            src_ref=kvb.at[:, 4 * w + (to ^ (1 << d)), 0, part],
            dst_ref=kvb.at[:, 4 * w + to, 0, part],
            send_sem=k_s.at[i], recv_sem=k_r.at[i], device_id=kn[d], device_id_type=MESH)

    kmsg = [{(t, to): kroute(w, t, to) for t in range(2) for to in range(1, 4)} for w in range(2)]
    smsg = [pltpu.make_async_remote_copy(
        src_ref=kvb.at[:, i, 0], dst_ref=kvb.at[:, i, 1], send_sem=s_s.at[i],
        recv_sem=s_r.at[i], device_id=sib, device_id_type=MESH) for i in range(8)]

    def kbegin(w):
        for t in range(2):
            kmsg[w][t, 1 << t].start()
        for t in range(2):
            kmsg[w][t, 2 >> t].start()
        smsg[4 * w].start()

    def kpass(w):
        for t in range(2):
            kmsg[w][t, 1 << t].wait_recv()
            kmsg[w][t, 3].start()

    def knear(w):
        for t in range(2):
            kmsg[w][t, 2 >> t].wait_recv()
        smsg[4 * w + 1].start()
        smsg[4 * w + 2].start()

    def kfar(w):
        for t in range(2):
            kmsg[w][t, 3].wait_recv()
        smsg[4 * w + 3].start()

    root = 1.0 / math.sqrt(DH)
    base2 = root * math.log2(math.e)

    def prep_k(first, count):
        for i in range(first, first + count):
            smsg[i].wait_recv()

        def one(i, _):
            r = pl.ds(pl.multiple_of(i * 256, 256), 256)
            kh, km, kl = three(kvb[0, i].reshape(256, DH))
            dh, dm = two(kvb[1, i].reshape(256, DH))
            ks[r, :] = jnp.concatenate([kh, km, kh, km, kl, kh], axis=1)
            ky[r, :] = jnp.concatenate([kh, dh, km, dm, kh, dh], axis=1)
            for a in range(2):
                hi, lo = two(jnp.transpose(kvb[2 + a, i].reshape(256, DH)))
                vh[a * DH:(a + 1) * DH, r] = hi
                vl[a * DH:(a + 1) * DH, r] = lo
            return 0
        lax.fori_loop(first, first + count, one, 0)

    def prep_q(first, count):
        def one(i, _):
            r = pl.ds(pl.multiple_of(i * LN, LN), LN)
            raw = qb[0, i]
            h, m, l = three(raw * base2)
            qs[r, :] = jnp.concatenate([h, h, m, m, h, l], axis=1)
            h, m = two(raw * root)
            dh, dm = two(qb[1, i] * root)
            qx[r, :] = jnp.concatenate([dh, h, dh, h, dm, m], axis=1)
            ac[i] = jnp.zeros(ac.shape[1:], F32)
            ac[i, 88:89, :] = jnp.full((1, LN), -1e30, F32)
            return 0
        lax.fori_loop(first, first + count, one, 0)

    def tile(at, k0, keys):
        first = at * 4
        r = pl.ds(pl.multiple_of(first * LN, 4 * LN), 4 * LN)
        c = slice(k0 * 256, (k0 + keys) * 256)

        def lanes(row):
            return jnp.concatenate([ac[first + i, row:row + 1, :] for i in range(4)], axis=1)

        s = nt(ks[c, :], qs[r, :])
        t = nt(ky[c, :], qx[r, :])
        old = lanes(88)
        peak = jnp.maximum(old, jnp.max(s, axis=0, keepdims=True))
        fade = jnp.exp2(old - peak)
        e = jnp.exp2(s - peak)
        w = e * t
        total = lanes(89) * fade + jnp.sum(e, axis=0, keepdims=True)
        total_t = lanes(90) * fade + jnp.sum(w, axis=0, keepdims=True)
        eh, el = two(e)
        wh, wl = two(w)
        hi, lo = vh[:, c], vl[:, c]
        n = nn(hi, eh) + nn(lo, eh) + nn(hi, el)
        u = nn(hi[:DH], wh) + nn(lo[:DH], wh) + nn(hi[:DH], wl)
        tan = n[DH:] + u
        for i in range(4):
            s_ = slice(i * LN, (i + 1) * LN)
            f = fade[:, s_]
            p = first + i
            ac[p, 0:88, :] = ac[p, 0:88, :] * f + n[0:88, s_]
            ac[p, 96:136, :] = ac[p, 96:136, :] * f + n[88:128, s_]
            ac[p, 136:184, :] = ac[p, 136:184, :] * f + tan[0:48, s_]
            ac[p, 192:272, :] = ac[p, 192:272, :] * f + tan[48:128, s_]
            ac[p, 88:89, :] = peak[:, s_]
            ac[p, 89:90, :] = total[:, s_]
            ac[p, 90:91, :] = total_t[:, s_]

    def sweep(first, count, k0, keys):
        def one(i, _):
            tile(first + i, k0, keys)
            return 0
        lax.fori_loop(0, count, one, 0)

    def bmsg(w, t, src, d, i):
        r0, n = PART[t]
        j = w * 21 + t * 7 + i
        return pltpu.make_async_remote_copy(
            src_ref=ac.at[8 * w + POS[src], pl.ds(r0, n)], dst_ref=rb.at[w, t, i, pl.ds(0, n)],
            send_sem=b_s.at[j], recv_sem=b_r.at[j], device_id=qn[d], device_id_type=MESH)

    back = {}
    for w in range(2):
        for t in range(3):
            a, b, c = names(t)
            for i, to in enumerate((0, a, b, a | b)):
                back[w, t, 1, to] = bmsg(w, t, to | c, (t + 2) % 3, i)
            for i, to in enumerate((0, a)):
                back[w, t, 2, to] = bmsg(w, t, to | b, (t + 1) % 3, 4 + i)
            back[w, t, 3, 0] = bmsg(w, t, a, t, 6)

    def leave(at):
        for p in range(at * 4 + 3, at * 4 - 1, -1):
            ac[p, 184:192, :] = ac[p, 88:96, :]
            ac[p, 272:280, :] = ac[p, 88:96, :]
            w, r = p // 8, ORDER[p % 8]
            for t in range(3):
                c = names(t)[2]
                if r & c:
                    back[w, t, 1, r ^ c].start()

    def merge(w, t, step, to):
        back[w, t, step, to].wait_recv()
        a, b, _ = names(t)
        i = {1: {0: 0, a: 1, b: 2, a | b: 3}, 2: {0: 4, a: 5}, 3: {0: 6}}[step][to]
        r0, n = PART[t]
        st, p = STAT[t], 8 * w + POS[to]
        m1, m2 = ac[p, st:st + 1, :], rb[w, t, i, n - 8:n - 7, :]
        top = jnp.maximum(m1, m2)
        f1, f2 = jnp.exp2(m1 - top), jnp.exp2(m2 - top)
        ac[p, r0:r0 + n, :] = ac[p, r0:r0 + n, :] * f1 + rb[w, t, i, :n, :] * f2
        ac[p, st:st + 1, :] = top

    def back_far(w):
        for t in range(3):
            a, b, c = names(t)
            merge(w, t, 1, a | b)
            back[w, t, 2, a].start()

    def back_near(w):
        for t in range(3):
            a, b, c = names(t)
            merge(w, t, 1, b)
            back[w, t, 2, 0].start()
        for t in range(3):
            a, b, c = names(t)
            merge(w, t, 1, a)
            merge(w, t, 2, a)
            back[w, t, 3, 0].start()

    def back_three(w):
        for t in range(3):
            merge(w, t, 1, 0)
            merge(w, t, 2, 0)
        for t in range(3):
            merge(w, t, 3, 0)
        p = 8 * w
        inv = [1.0 / ac[p, s + 1:s + 2, :] for s in STAT]
        rt = [ac[p, s + 2:s + 3, :] for s in STAT]
        att = jnp.concatenate([ac[p, 0:88, :] * inv[0], ac[p, 96:136, :] * inv[1]], axis=0)
        tan = jnp.concatenate([
            (ac[p, 136:184, :] - att[0:48] * rt[1]) * inv[1],
            (ac[p, 192:272, :] - att[48:128] * rt[2]) * inv[2],
        ], axis=0)
        fin[w, 0] = jnp.transpose(att)
        fin[w, 1] = jnp.transpose(tan)

    outs = [pltpu.make_async_copy(fin.at[0, i], out.at[:, mine], f_o.at[i])
            for i, out in enumerate((o, ot))]
    gifts = [pltpu.make_async_remote_copy(
        src_ref=fin.at[1, i], dst_ref=out.at[:, mine], send_sem=f_s.at[i],
        recv_sem=f_r.at[i], device_id=mate, device_id_type=MESH)
        for i, out in enumerate((o, ot))]

    for c in owns:
        c.wait()
    begin(qmsg[0])
    kbegin(0)
    prep_q(0, 1)
    pass_first(qmsg[0])
    prep_k(0, 1)
    pass_second(qmsg[0])
    kpass(0)
    end_near(qmsg[0])
    prep_q(1, 3)
    pass_both(qmsg[0])
    for i in range(2):
        swaps[i].wait_recv()
    begin(qmsg[1])
    tile(0, 0, 1)
    knear(0)
    for i in range(2, 6):
        swaps[i].wait_recv()
    kbegin(1)
    prep_k(1, 2)
    tile(0, 1, 2)
    pass_first(qmsg[1])
    end_far(qmsg[0])
    prep_q(4, 4)
    kfar(0)
    tile(1, 0, 3)
    pass_second(qmsg[1])
    kpass(1)
    pass_both(qmsg[1])
    prep_k(3, 2)
    sweep(0, 2, 3, 2)
    knear(1)
    end_near(qmsg[1])
    end_far(qmsg[1])
    prep_q(8, 8)
    tile(3, 0, 3)
    kfar(1)
    tile(3, 3, 2)
    prep_k(5, 3)
    tile(3, 5, 3)
    leave(3)
    tile(1, 5, 3)
    leave(1)
    tile(2, 0, 5)
    back_far(1)
    tile(2, 5, 3)
    leave(2)
    back_far(0)
    back_near(1)
    tile(0, 5, 3)
    leave(0)
    back_near(0)
    back_three(1)
    for c in gifts:
        c.start()
    back_three(0)
    for c in outs:
        c.start()
    for c in outs + gifts:
        c.wait()
    for c in swaps + smsg:
        c.wait_send()
    for m in kmsg + qmsg + [back]:
        for c in m.values():
            c.wait_send()


def per_device(queries, keys, values, query_tangent, key_tangent, value_tangent):
    hbm = pl.BlockSpec(memory_space=pl.ANY)
    dma = pltpu.SemaphoreType.DMA
    shape = jax.ShapeDtypeStruct((2,) + queries.shape, F32)
    both = pl.pallas_call(
        kernel,
        out_shape=shape,
        in_specs=[hbm] * 6,
        out_specs=hbm,
        scratch_shapes=[
            pltpu.VMEM((4, 8, 2, LN, DH), F32),
            pltpu.VMEM((2, 16, LN, DH), F32),
            pltpu.VMEM((2048, 768), BF),
            pltpu.VMEM((2048, 768), BF),
            pltpu.VMEM((256, 2048), BF),
            pltpu.VMEM((256, 2048), BF),
            pltpu.VMEM((2048, 768), BF),
            pltpu.VMEM((2048, 768), BF),
            pltpu.VMEM((16, 280, LN), F32),
            pltpu.VMEM((2, 3, 7, 96, LN), F32),
            pltpu.VMEM((2, 2, LN, DH), F32),
            dma((6,)), dma((6,)), dma((6,)),
            dma((16,)), dma((16,)), dma((48,)), dma((48,)),
            dma((8,)), dma((8,)), dma((42,)), dma((42,)),
            dma((2,)), dma((2,)), dma((2,)),
        ],
        compiler_params=pltpu.CompilerParams(
            collective_id=0, has_side_effects=True, vmem_limit_bytes=62 << 20
        ),
        name="attention_tangent",
    )(queries, query_tangent, keys, key_tangent, values, value_tangent)
    return both[0], both[1]


def solution(mesh):
    spec = P(("pb", "kv"), None)
    return jax.shard_map(
        per_device, mesh=mesh, in_specs=(spec,) * 6, out_specs=(spec, spec), check_vma=False
    )
```

```python
import math

import jax
import jax.numpy as jnp
from jax import lax
from jax.experimental import pallas as pl
from jax.experimental.pallas import tpu as pltpu
from jax.sharding import PartitionSpec as P

DH = 128
LN = 128
F32, BF = jnp.float32, jnp.bfloat16
MESH = pl.DeviceIdType.MESH
ORDER = (0, 1, 2, 4, 3, 5, 6, 7)
POS = tuple(ORDER.index(r) for r in range(8))
THIRD = (((0, 48), (48, 40), (88, 40)), ((0, 40), (40, 48), (88, 40)))
PART = ((0, 96), (96, 96), (192, 88))
STAT = (88, 184, 272)


def nt(a, b):
    return lax.dot_general(a, b, (((1,), (1,)), ((), ())), preferred_element_type=F32)


def nn(a, b):
    return jnp.dot(a, b, preferred_element_type=F32)


def two(x):
    hi = x.astype(BF)
    return hi, (x - hi.astype(F32)).astype(BF)


def kernel(q, dq, k, dk, v, dv, oo, kvb, qb, ks, ky, vh, vl, qs, qx, ac, rb, fin,
           swap_s, swap_r, own_s, k_s, k_r, q_s, q_r, s_s, s_r, b_s, b_r, f_s, f_r, f_o):
    o, ot = oo.at[0], oo.at[1]
    pb, kv = lax.axis_index("pb"), lax.axis_index("kv")
    core, x = pb % 2, pb // 4
    z, y = (kv // 4) * 2 + (pb // 2) % 2, kv % 4
    head = ((z + 1) // 2) % 2

    def dev(x, y, z, c):
        return (x * 4 + (z % 2) * 2 + c, (z // 2) * 4 + y)

    def near(i):
        return i + 1 - 2 * (i % 2)

    def far(i):
        return (i + 2 * (i % 2) + 3) % 4

    kn = (dev(near(x), y, z, core), dev(x, near(y), z, core))
    qn = (dev(far(x), y, z, core), dev(x, far(y), z, core), dev(x, y, far(z), core))
    mate = dev(x, y, near(z), core)
    sib = dev(x, y, z, 1 - core)

    barrier = pltpu.get_barrier_semaphore()
    for other in kn + qn + (mate, sib):
        pl.semaphore_signal(barrier, inc=1, device_id=other, device_id_type=MESH)
    mine = pl.ds(pl.multiple_of(head * DH, DH), DH)
    theirs = pl.ds(pl.multiple_of((1 - head) * DH, DH), DH)
    table = ((q, qb, 0), (dq, qb, 1), (k, kvb, 0), (dk, kvb, 1), (v, kvb, 2), (dv, kvb, 3))

    def place(dst, a, wave):
        return dst.at[a, 8 * wave] if dst is qb else dst.at[a, 4 * wave, 0]

    owns = [pltpu.make_async_copy(ref.at[:, mine], place(dst, a, 0), own_s.at[i])
            for i, (ref, dst, a) in enumerate(table)]
    for c in owns:
        c.start()
    pl.semaphore_wait(barrier, 7)
    swaps = [pltpu.make_async_remote_copy(
        src_ref=ref.at[:, theirs], dst_ref=place(dst, a, 1), send_sem=swap_s.at[i],
        recv_sem=swap_r.at[i], device_id=mate, device_id_type=MESH)
        for i, (ref, dst, a) in enumerate(table)]
    for c in swaps:
        c.start()

    def names(t):
        return 1 << t, 1 << (t + 1) % 3, 1 << (t + 2) % 3

    def qroute(w, t, to):
        d = [i for i in ((t + j) % 3 for j in range(3)) if to >> i & 1][-1]
        part = pl.ds(*THIRD[w][t])
        i = w * 24 + t * 8 + to
        return pltpu.make_async_remote_copy(
            src_ref=qb.at[:, 8 * w + POS[to ^ (1 << d)], part],
            dst_ref=qb.at[:, 8 * w + POS[to], part],
            send_sem=q_s.at[i], recv_sem=q_r.at[i], device_id=qn[d], device_id_type=MESH)

    qmsg = [{(t, to): qroute(w, t, to) for t in range(3) for to in range(1, 8)} for w in range(2)]

    def begin(m):
        for step in range(3):
            for t in range(3):
                m[t, names(t)[step]].start()

    def pass_first(m):
        for t in range(3):
            a, b, c = names(t)
            m[t, a].wait_recv()
            m[t, a | b].start()
            m[t, a | c].start()

    def pass_second(m):
        for t in range(3):
            a, b, c = names(t)
            m[t, b].wait_recv()
            m[t, b | c].start()

    def pass_both(m):
        for t in range(3):
            a, b, c = names(t)
            m[t, a | b].wait_recv()
            m[t, a | b | c].start()

    def end_near(m):
        for t in range(3):
            m[t, names(t)[2]].wait_recv()

    def end_far(m):
        for t in range(3):
            a, b, c = names(t)
            for to in (a | c, b | c, a | b | c):
                m[t, to].wait_recv()

    def kroute(w, t, to):
        d = 1 - t if to >> (1 - t) & 1 else t
        part = pl.ds(64 * t, 64)
        i = w * 8 + t * 4 + to
        return pltpu.make_async_remote_copy(
            src_ref=kvb.at[:, 4 * w + (to ^ (1 << d)), 0, part],
            dst_ref=kvb.at[:, 4 * w + to, 0, part],
            send_sem=k_s.at[i], recv_sem=k_r.at[i], device_id=kn[d], device_id_type=MESH)

    kmsg = [{(t, to): kroute(w, t, to) for t in range(2) for to in range(1, 4)} for w in range(2)]
    smsg = [pltpu.make_async_remote_copy(
        src_ref=kvb.at[:, i, 0], dst_ref=kvb.at[:, i, 1], send_sem=s_s.at[i],
        recv_sem=s_r.at[i], device_id=sib, device_id_type=MESH) for i in range(8)]

    def kbegin(w):
        for t in range(2):
            kmsg[w][t, 1 << t].start()
        for t in range(2):
            kmsg[w][t, 2 >> t].start()
        smsg[4 * w].start()

    def kpass(w):
        for t in range(2):
            kmsg[w][t, 1 << t].wait_recv()
            kmsg[w][t, 3].start()

    def knear(w):
        for t in range(2):
            kmsg[w][t, 2 >> t].wait_recv()
        smsg[4 * w + 1].start()
        smsg[4 * w + 2].start()

    def kfar(w):
        for t in range(2):
            kmsg[w][t, 3].wait_recv()
        smsg[4 * w + 3].start()

    root = 1.0 / math.sqrt(DH)
    base2 = root * math.log2(math.e)

    def prep_k(first, count):
        for i in range(first, first + count):
            smsg[i].wait_recv()

        def one(i, _):
            r = pl.ds(pl.multiple_of(i * 256, 256), 256)
            kh, km = two(kvb[0, i].reshape(256, DH))
            dh, dm = two(kvb[1, i].reshape(256, DH))
            ks[r, :] = jnp.concatenate([kh, km, kh, km], axis=1)
            ky[r, :] = jnp.concatenate([kh, dh, km, dm, kh, dh], axis=1)
            for a in range(2):
                hi, lo = two(jnp.transpose(kvb[2 + a, i].reshape(256, DH)))
                vh[a * DH:(a + 1) * DH, r] = hi
                vl[a * DH:(a + 1) * DH, r] = lo
            return 0
        lax.fori_loop(first, first + count, one, 0)

    def prep_q(first, count):
        def one(i, _):
            r = pl.ds(pl.multiple_of(i * LN, LN), LN)
            raw = qb[0, i]
            h, m = two(raw * base2)
            qs[r, :] = jnp.concatenate([h, h, m, m], axis=1)
            h, m = two(raw * root)
            dh, dm = two(qb[1, i] * root)
            qx[r, :] = jnp.concatenate([dh, h, dh, h, dm, m], axis=1)
            ac[i] = jnp.zeros(ac.shape[1:], F32)
            ac[i, 88:89, :] = jnp.full((1, LN), -1e30, F32)
            return 0
        lax.fori_loop(first, first + count, one, 0)

    def tile(at, k0, keys):
        first = at * 4
        r = pl.ds(pl.multiple_of(first * LN, 4 * LN), 4 * LN)
        c = slice(k0 * 256, (k0 + keys) * 256)

        def lanes(row):
            return jnp.concatenate([ac[first + i, row:row + 1, :] for i in range(4)], axis=1)

        s = nt(ks[c, :], qs[r, :])
        t = nt(ky[c, :], qx[r, :])
        old = lanes(88)
        peak = jnp.maximum(old, jnp.max(s, axis=0, keepdims=True))
        fade = jnp.exp2(old - peak)
        e = jnp.exp2(s - peak)
        w = e * t
        total = lanes(89) * fade + jnp.sum(e, axis=0, keepdims=True)
        total_t = lanes(90) * fade + jnp.sum(w, axis=0, keepdims=True)
        eh, el = two(e)
        wh, wl = two(w)
        hi, lo = vh[:, c], vl[:, c]
        n = nn(hi, eh) + nn(lo, eh) + nn(hi, el)
        u = nn(hi[:DH], wh) + nn(lo[:DH], wh) + nn(hi[:DH], wl)
        tan = n[DH:] + u
        for i in range(4):
            s_ = slice(i * LN, (i + 1) * LN)
            f = fade[:, s_]
            p = first + i
            ac[p, 0:88, :] = ac[p, 0:88, :] * f + n[0:88, s_]
            ac[p, 96:136, :] = ac[p, 96:136, :] * f + n[88:128, s_]
            ac[p, 136:184, :] = ac[p, 136:184, :] * f + tan[0:48, s_]
            ac[p, 192:272, :] = ac[p, 192:272, :] * f + tan[48:128, s_]
            ac[p, 88:89, :] = peak[:, s_]
            ac[p, 89:90, :] = total[:, s_]
            ac[p, 90:91, :] = total_t[:, s_]

    def sweep(first, count, k0, keys):
        def one(i, _):
            tile(first + i, k0, keys)
            return 0
        lax.fori_loop(0, count, one, 0)

    def bmsg(w, t, src, d, i):
        r0, n = PART[t]
        j = w * 21 + t * 7 + i
        return pltpu.make_async_remote_copy(
            src_ref=ac.at[8 * w + POS[src], pl.ds(r0, n)], dst_ref=rb.at[w, t, i, pl.ds(0, n)],
            send_sem=b_s.at[j], recv_sem=b_r.at[j], device_id=qn[d], device_id_type=MESH)

    back = {}
    for w in range(2):
        for t in range(3):
            a, b, c = names(t)
            for i, to in enumerate((0, a, b, a | b)):
                back[w, t, 1, to] = bmsg(w, t, to | c, (t + 2) % 3, i)
            for i, to in enumerate((0, a)):
                back[w, t, 2, to] = bmsg(w, t, to | b, (t + 1) % 3, 4 + i)
            back[w, t, 3, 0] = bmsg(w, t, a, t, 6)

    def leave(at):
        for p in range(at * 4 + 3, at * 4 - 1, -1):
            ac[p, 184:192, :] = ac[p, 88:96, :]
            ac[p, 272:280, :] = ac[p, 88:96, :]
            w, r = p // 8, ORDER[p % 8]
            for t in range(3):
                c = names(t)[2]
                if r & c:
                    back[w, t, 1, r ^ c].start()

    def merge(w, t, step, to):
        back[w, t, step, to].wait_recv()
        a, b, _ = names(t)
        i = {1: {0: 0, a: 1, b: 2, a | b: 3}, 2: {0: 4, a: 5}, 3: {0: 6}}[step][to]
        r0, n = PART[t]
        st, p = STAT[t], 8 * w + POS[to]
        m1, m2 = ac[p, st:st + 1, :], rb[w, t, i, n - 8:n - 7, :]
        top = jnp.maximum(m1, m2)
        f1, f2 = jnp.exp2(m1 - top), jnp.exp2(m2 - top)
        ac[p, r0:r0 + n, :] = ac[p, r0:r0 + n, :] * f1 + rb[w, t, i, :n, :] * f2
        ac[p, st:st + 1, :] = top

    def back_far(w):
        for t in range(3):
            a, b, c = names(t)
            merge(w, t, 1, a | b)
            back[w, t, 2, a].start()

    def back_near(w):
        for t in range(3):
            a, b, c = names(t)
            merge(w, t, 1, b)
            back[w, t, 2, 0].start()
        for t in range(3):
            a, b, c = names(t)
            merge(w, t, 1, a)
            merge(w, t, 2, a)
            back[w, t, 3, 0].start()

    def back_three(w):
        for t in range(3):
            merge(w, t, 1, 0)
            merge(w, t, 2, 0)
        for t in range(3):
            merge(w, t, 3, 0)
        p = 8 * w
        inv = [1.0 / ac[p, s + 1:s + 2, :] for s in STAT]
        rt = [ac[p, s + 2:s + 3, :] for s in STAT]
        att = jnp.concatenate([ac[p, 0:88, :] * inv[0], ac[p, 96:136, :] * inv[1]], axis=0)
        tan = jnp.concatenate([
            (ac[p, 136:184, :] - att[0:48] * rt[1]) * inv[1],
            (ac[p, 192:272, :] - att[48:128] * rt[2]) * inv[2],
        ], axis=0)
        fin[w, 0] = jnp.transpose(att)
        fin[w, 1] = jnp.transpose(tan)

    outs = [pltpu.make_async_copy(fin.at[0, i], out.at[:, mine], f_o.at[i])
            for i, out in enumerate((o, ot))]
    gifts = [pltpu.make_async_remote_copy(
        src_ref=fin.at[1, i], dst_ref=out.at[:, mine], send_sem=f_s.at[i],
        recv_sem=f_r.at[i], device_id=mate, device_id_type=MESH)
        for i, out in enumerate((o, ot))]

    for c in owns:
        c.wait()
    begin(qmsg[0])
    kbegin(0)
    prep_q(0, 1)
    pass_first(qmsg[0])
    prep_k(0, 1)
    pass_second(qmsg[0])
    kpass(0)
    end_near(qmsg[0])
    prep_q(1, 3)
    pass_both(qmsg[0])
    for i in range(2):
        swaps[i].wait_recv()
    begin(qmsg[1])
    tile(0, 0, 1)
    knear(0)
    for i in range(2, 6):
        swaps[i].wait_recv()
    kbegin(1)
    prep_k(1, 2)
    tile(0, 1, 2)
    pass_first(qmsg[1])
    end_far(qmsg[0])
    prep_q(4, 4)
    kfar(0)
    tile(1, 0, 3)
    pass_second(qmsg[1])
    kpass(1)
    pass_both(qmsg[1])
    prep_k(3, 2)
    sweep(0, 2, 3, 2)
    knear(1)
    end_near(qmsg[1])
    end_far(qmsg[1])
    prep_q(8, 8)
    tile(3, 0, 3)
    kfar(1)
    tile(3, 3, 2)
    prep_k(5, 3)
    tile(3, 5, 3)
    leave(3)
    tile(1, 5, 3)
    leave(1)
    tile(2, 0, 5)
    back_far(1)
    tile(2, 5, 3)
    leave(2)
    back_far(0)
    back_near(1)
    tile(0, 5, 3)
    leave(0)
    back_near(0)
    back_three(1)
    for c in gifts:
        c.start()
    back_three(0)
    for c in outs:
        c.start()
    for c in outs + gifts:
        c.wait()
    for c in swaps + smsg:
        c.wait_send()
    for m in kmsg + qmsg + [back]:
        for c in m.values():
            c.wait_send()


def per_device(queries, keys, values, query_tangent, key_tangent, value_tangent):
    hbm = pl.BlockSpec(memory_space=pl.ANY)
    dma = pltpu.SemaphoreType.DMA
    shape = jax.ShapeDtypeStruct((2,) + queries.shape, F32)
    both = pl.pallas_call(
        kernel,
        out_shape=shape,
        in_specs=[hbm] * 6,
        out_specs=hbm,
        scratch_shapes=[
            pltpu.VMEM((4, 8, 2, LN, DH), F32),
            pltpu.VMEM((2, 16, LN, DH), F32),
            pltpu.VMEM((2048, 512), BF),
            pltpu.VMEM((2048, 768), BF),
            pltpu.VMEM((256, 2048), BF),
            pltpu.VMEM((256, 2048), BF),
            pltpu.VMEM((2048, 512), BF),
            pltpu.VMEM((2048, 768), BF),
            pltpu.VMEM((16, 280, LN), F32),
            pltpu.VMEM((2, 3, 7, 96, LN), F32),
            pltpu.VMEM((2, 2, LN, DH), F32),
            dma((6,)), dma((6,)), dma((6,)),
            dma((16,)), dma((16,)), dma((48,)), dma((48,)),
            dma((8,)), dma((8,)), dma((42,)), dma((42,)),
            dma((2,)), dma((2,)), dma((2,)),
        ],
        compiler_params=pltpu.CompilerParams(
            collective_id=0, has_side_effects=True, vmem_limit_bytes=62 << 20
        ),
        name="attention_tangent",
    )(queries, query_tangent, keys, key_tangent, values, value_tangent)
    return both[0], both[1]


def solution(mesh):
    spec = P(("pb", "kv"), None)
    return jax.shard_map(
        per_device, mesh=mesh, in_specs=(spec,) * 6, out_specs=(spec, spec), check_vma=False
    )
```

```python
import math

import jax
import jax.numpy as jnp
from jax import lax
from jax.experimental import pallas as pl
from jax.experimental.pallas import tpu as pltpu
from jax.sharding import PartitionSpec as P

DH = 128
LN = 128
F32, BF = jnp.float32, jnp.bfloat16
MESH = pl.DeviceIdType.MESH
ORDER = (0, 1, 2, 4, 3, 5, 6, 7)
POS = tuple(ORDER.index(r) for r in range(8))
THIRD = (((0, 48), (48, 40), (88, 40)), ((0, 40), (40, 48), (88, 40)))
PART = ((0, 96), (96, 96), (192, 88))
STAT = (88, 184, 272)


def nt(a, b):
    return lax.dot_general(a, b, (((1,), (1,)), ((), ())), preferred_element_type=F32)


def nn(a, b):
    return jnp.dot(a, b, preferred_element_type=F32)


def two(x):
    hi = x.astype(BF)
    return hi, (x - hi.astype(F32)).astype(BF)


def kernel(q, dq, k, dk, v, dv, oo, kvb, qb, ks, ky, vh, vl, qs, qx, ac, rb, fin,
           swap_s, swap_r, own_s, k_s, k_r, q_s, q_r, s_s, s_r, b_s, b_r, f_s, f_r, f_o):
    o, ot = oo.at[0], oo.at[1]
    pb, kv = lax.axis_index("pb"), lax.axis_index("kv")
    core, x = pb % 2, pb // 4
    z, y = (kv // 4) * 2 + (pb // 2) % 2, kv % 4
    head = ((z + 1) // 2) % 2

    def dev(x, y, z, c):
        return (x * 4 + (z % 2) * 2 + c, (z // 2) * 4 + y)

    def near(i):
        return i + 1 - 2 * (i % 2)

    def far(i):
        return (i + 2 * (i % 2) + 3) % 4

    kn = (dev(near(x), y, z, core), dev(x, near(y), z, core))
    qn = (dev(far(x), y, z, core), dev(x, far(y), z, core), dev(x, y, far(z), core))
    mate = dev(x, y, near(z), core)
    sib = dev(x, y, z, 1 - core)

    barrier = pltpu.get_barrier_semaphore()
    for other in kn + qn + (mate, sib):
        pl.semaphore_signal(barrier, inc=1, device_id=other, device_id_type=MESH)
    mine = pl.ds(pl.multiple_of(head * DH, DH), DH)
    theirs = pl.ds(pl.multiple_of((1 - head) * DH, DH), DH)
    table = ((q, qb, 0), (dq, qb, 1), (k, kvb, 0), (dk, kvb, 1), (v, kvb, 2), (dv, kvb, 3))

    def place(dst, a, wave):
        return dst.at[a, 8 * wave] if dst is qb else dst.at[a, 4 * wave, 0]

    owns = [pltpu.make_async_copy(ref.at[:, mine], place(dst, a, 0), own_s.at[i])
            for i, (ref, dst, a) in enumerate(table)]
    for c in owns:
        c.start()
    pl.semaphore_wait(barrier, 7)
    swaps = [pltpu.make_async_remote_copy(
        src_ref=ref.at[:, theirs], dst_ref=place(dst, a, 1), send_sem=swap_s.at[i],
        recv_sem=swap_r.at[i], device_id=mate, device_id_type=MESH)
        for i, (ref, dst, a) in enumerate(table)]
    for c in swaps:
        c.start()

    def names(t):
        return 1 << t, 1 << (t + 1) % 3, 1 << (t + 2) % 3

    def qroute(w, t, to):
        d = [i for i in ((t + j) % 3 for j in range(3)) if to >> i & 1][-1]
        part = pl.ds(*THIRD[w][t])
        i = w * 24 + t * 8 + to
        return pltpu.make_async_remote_copy(
            src_ref=qb.at[:, 8 * w + POS[to ^ (1 << d)], part],
            dst_ref=qb.at[:, 8 * w + POS[to], part],
            send_sem=q_s.at[i], recv_sem=q_r.at[i], device_id=qn[d], device_id_type=MESH)

    qmsg = [{(t, to): qroute(w, t, to) for t in range(3) for to in range(1, 8)} for w in range(2)]

    def begin(m):
        for step in range(3):
            for t in range(3):
                m[t, names(t)[step]].start()

    def pass_first(m):
        for t in range(3):
            a, b, c = names(t)
            m[t, a].wait_recv()
            m[t, a | b].start()
            m[t, a | c].start()

    def pass_second(m):
        for t in range(3):
            a, b, c = names(t)
            m[t, b].wait_recv()
            m[t, b | c].start()

    def pass_both(m):
        for t in range(3):
            a, b, c = names(t)
            m[t, a | b].wait_recv()
            m[t, a | b | c].start()

    def end_near(m):
        for t in range(3):
            m[t, names(t)[2]].wait_recv()

    def end_far(m):
        for t in range(3):
            a, b, c = names(t)
            for to in (a | c, b | c, a | b | c):
                m[t, to].wait_recv()

    def kroute(w, t, to):
        d = 1 - t if to >> (1 - t) & 1 else t
        part = pl.ds(64 * t, 64)
        i = w * 8 + t * 4 + to
        return pltpu.make_async_remote_copy(
            src_ref=kvb.at[:, 4 * w + (to ^ (1 << d)), 0, part],
            dst_ref=kvb.at[:, 4 * w + to, 0, part],
            send_sem=k_s.at[i], recv_sem=k_r.at[i], device_id=kn[d], device_id_type=MESH)

    kmsg = [{(t, to): kroute(w, t, to) for t in range(2) for to in range(1, 4)} for w in range(2)]
    def handed(i, t):
        part = pl.ds(64 * t, 64)
        return pltpu.make_async_remote_copy(
            src_ref=kvb.at[:, i, 0, part], dst_ref=kvb.at[:, i, 1, part],
            send_sem=s_s.at[2 * i + t], recv_sem=s_r.at[2 * i + t],
            device_id=sib, device_id_type=MESH)

    smsg = [[handed(i, t) for t in range(2)] for i in range(8)]

    def kbegin(w):
        for t in range(2):
            kmsg[w][t, 1 << t].start()
        for t in range(2):
            kmsg[w][t, 2 >> t].start()
        for c in smsg[4 * w]:
            c.start()

    def kpass(w):
        for t in range(2):
            kmsg[w][t, 1 << t].wait_recv()
            kmsg[w][t, 3].start()
            smsg[4 * w + (1 << t)][t].start()

    def knear(w):
        for t in range(2):
            kmsg[w][t, 2 >> t].wait_recv()
            smsg[4 * w + (2 >> t)][t].start()

    def kfar(w):
        for t in range(2):
            kmsg[w][t, 3].wait_recv()
            smsg[4 * w + 3][t].start()

    root = 1.0 / math.sqrt(DH)
    base2 = root * math.log2(math.e)

    def prep_k(first, count):
        for i in range(first, first + count):
            for c in smsg[i]:
                c.wait_recv()

        def one(i, _):
            r = pl.ds(pl.multiple_of(i * 256, 256), 256)
            kh, km = two(kvb[0, i].reshape(256, DH))
            dh, dm = two(kvb[1, i].reshape(256, DH))
            ks[r, :] = jnp.concatenate([kh, km, kh, km], axis=1)
            ky[r, :] = jnp.concatenate([kh, dh, km, dm, kh, dh], axis=1)
            for a in range(2):
                hi, lo = two(jnp.transpose(kvb[2 + a, i].reshape(256, DH)))
                vh[a * DH:(a + 1) * DH, r] = hi
                vl[a * DH:(a + 1) * DH, r] = lo
            return 0
        lax.fori_loop(first, first + count, one, 0)

    def prep_q(first, count):
        def one(i, _):
            r = pl.ds(pl.multiple_of(i * LN, LN), LN)
            raw = qb[0, i]
            h, m = two(raw * base2)
            qs[r, :] = jnp.concatenate([h, h, m, m], axis=1)
            h, m = two(raw * root)
            dh, dm = two(qb[1, i] * root)
            qx[r, :] = jnp.concatenate([dh, h, dh, h, dm, m], axis=1)
            ac[i] = jnp.zeros(ac.shape[1:], F32)
            ac[i, 88:89, :] = jnp.full((1, LN), -1e30, F32)
            return 0
        lax.fori_loop(first, first + count, one, 0)

    def tile(at, k0, keys):
        first = at * 4
        r = pl.ds(pl.multiple_of(first * LN, 4 * LN), 4 * LN)
        c = slice(k0 * 256, (k0 + keys) * 256)

        def lanes(row):
            return jnp.concatenate([ac[first + i, row:row + 1, :] for i in range(4)], axis=1)

        s = nt(ks[c, :], qs[r, :])
        t = nt(ky[c, :], qx[r, :])
        old = lanes(88)
        peak = jnp.maximum(old, jnp.max(s, axis=0, keepdims=True))
        fade = jnp.exp2(old - peak)
        e = jnp.exp2(s - peak)
        w = e * t
        total = lanes(89) * fade + jnp.sum(e, axis=0, keepdims=True)
        total_t = lanes(90) * fade + jnp.sum(w, axis=0, keepdims=True)
        eh, el = two(e)
        wh, wl = two(w)
        hi, lo = vh[:, c], vl[:, c]
        n = nn(hi, eh) + nn(lo, eh) + nn(hi, el)
        u = nn(hi[:DH], wh) + nn(lo[:DH], wh) + nn(hi[:DH], wl)
        tan = n[DH:] + u
        for i in range(4):
            s_ = slice(i * LN, (i + 1) * LN)
            f = fade[:, s_]
            p = first + i
            ac[p, 0:88, :] = ac[p, 0:88, :] * f + n[0:88, s_]
            ac[p, 96:136, :] = ac[p, 96:136, :] * f + n[88:128, s_]
            ac[p, 136:184, :] = ac[p, 136:184, :] * f + tan[0:48, s_]
            ac[p, 192:272, :] = ac[p, 192:272, :] * f + tan[48:128, s_]
            ac[p, 88:89, :] = peak[:, s_]
            ac[p, 89:90, :] = total[:, s_]
            ac[p, 90:91, :] = total_t[:, s_]

    def sweep(first, count, k0, keys):
        def one(i, _):
            tile(first + i, k0, keys)
            return 0
        lax.fori_loop(0, count, one, 0)

    def bmsg(w, t, src, d, i):
        r0, n = PART[t]
        j = w * 21 + t * 7 + i
        return pltpu.make_async_remote_copy(
            src_ref=ac.at[8 * w + POS[src], pl.ds(r0, n)], dst_ref=rb.at[w, t, i, pl.ds(0, n)],
            send_sem=b_s.at[j], recv_sem=b_r.at[j], device_id=qn[d], device_id_type=MESH)

    back = {}
    for w in range(2):
        for t in range(3):
            a, b, c = names(t)
            for i, to in enumerate((0, a, b, a | b)):
                back[w, t, 1, to] = bmsg(w, t, to | c, (t + 2) % 3, i)
            for i, to in enumerate((0, a)):
                back[w, t, 2, to] = bmsg(w, t, to | b, (t + 1) % 3, 4 + i)
            back[w, t, 3, 0] = bmsg(w, t, a, t, 6)

    def leave(at):
        for p in range(at * 4 + 3, at * 4 - 1, -1):
            ac[p, 184:192, :] = ac[p, 88:96, :]
            ac[p, 272:280, :] = ac[p, 88:96, :]
            w, r = p // 8, ORDER[p % 8]
            for t in range(3):
                c = names(t)[2]
                if r & c:
                    back[w, t, 1, r ^ c].start()

    def merge(w, t, step, to):
        back[w, t, step, to].wait_recv()
        a, b, _ = names(t)
        i = {1: {0: 0, a: 1, b: 2, a | b: 3}, 2: {0: 4, a: 5}, 3: {0: 6}}[step][to]
        r0, n = PART[t]
        st, p = STAT[t], 8 * w + POS[to]
        m1, m2 = ac[p, st:st + 1, :], rb[w, t, i, n - 8:n - 7, :]
        top = jnp.maximum(m1, m2)
        f1, f2 = jnp.exp2(m1 - top), jnp.exp2(m2 - top)
        ac[p, r0:r0 + n, :] = ac[p, r0:r0 + n, :] * f1 + rb[w, t, i, :n, :] * f2
        ac[p, st:st + 1, :] = top

    def back_far(w):
        for t in range(3):
            a, b, c = names(t)
            merge(w, t, 1, a | b)
            back[w, t, 2, a].start()

    def back_near(w):
        for t in range(3):
            a, b, c = names(t)
            merge(w, t, 1, b)
            back[w, t, 2, 0].start()
        for t in range(3):
            a, b, c = names(t)
            merge(w, t, 1, a)
            merge(w, t, 2, a)
            back[w, t, 3, 0].start()

    def back_three(w):
        for t in range(3):
            merge(w, t, 1, 0)
            merge(w, t, 2, 0)
        for t in range(3):
            merge(w, t, 3, 0)
        p = 8 * w
        inv = [1.0 / ac[p, s + 1:s + 2, :] for s in STAT]
        rt = [ac[p, s + 2:s + 3, :] for s in STAT]
        att = jnp.concatenate([ac[p, 0:88, :] * inv[0], ac[p, 96:136, :] * inv[1]], axis=0)
        tan = jnp.concatenate([
            (ac[p, 136:184, :] - att[0:48] * rt[1]) * inv[1],
            (ac[p, 192:272, :] - att[48:128] * rt[2]) * inv[2],
        ], axis=0)
        fin[w, 0] = jnp.transpose(att)
        fin[w, 1] = jnp.transpose(tan)

    outs = [pltpu.make_async_copy(fin.at[0, i], out.at[:, mine], f_o.at[i])
            for i, out in enumerate((o, ot))]
    gifts = [pltpu.make_async_remote_copy(
        src_ref=fin.at[1, i], dst_ref=out.at[:, mine], send_sem=f_s.at[i],
        recv_sem=f_r.at[i], device_id=mate, device_id_type=MESH)
        for i, out in enumerate((o, ot))]

    for c in owns:
        c.wait()
    begin(qmsg[0])
    kbegin(0)
    prep_q(0, 1)
    pass_first(qmsg[0])
    prep_k(0, 1)
    pass_second(qmsg[0])
    kpass(0)
    end_near(qmsg[0])
    prep_q(1, 3)
    pass_both(qmsg[0])
    for i in range(2):
        swaps[i].wait_recv()
    begin(qmsg[1])
    tile(0, 0, 1)
    knear(0)
    for i in range(2, 6):
        swaps[i].wait_recv()
    kbegin(1)
    prep_k(1, 2)
    tile(0, 1, 2)
    pass_first(qmsg[1])
    end_far(qmsg[0])
    prep_q(4, 4)
    kfar(0)
    tile(1, 0, 3)
    pass_second(qmsg[1])
    kpass(1)
    pass_both(qmsg[1])
    prep_k(3, 2)
    sweep(0, 2, 3, 2)
    knear(1)
    end_near(qmsg[1])
    end_far(qmsg[1])
    prep_q(8, 8)
    tile(3, 0, 3)
    kfar(1)
    tile(3, 3, 2)
    prep_k(5, 3)
    tile(3, 5, 3)
    leave(3)
    tile(1, 5, 3)
    leave(1)
    tile(2, 0, 5)
    back_far(1)
    tile(2, 5, 3)
    leave(2)
    back_far(0)
    back_near(1)
    tile(0, 5, 3)
    leave(0)
    back_near(0)
    back_three(1)
    for c in gifts:
        c.start()
    back_three(0)
    for c in outs:
        c.start()
    for c in outs + gifts:
        c.wait()
    for c in swaps + sum(smsg, []):
        c.wait_send()
    for m in kmsg + qmsg + [back]:
        for c in m.values():
            c.wait_send()


def per_device(queries, keys, values, query_tangent, key_tangent, value_tangent):
    hbm = pl.BlockSpec(memory_space=pl.ANY)
    dma = pltpu.SemaphoreType.DMA
    shape = jax.ShapeDtypeStruct((2,) + queries.shape, F32)
    both = pl.pallas_call(
        kernel,
        out_shape=shape,
        in_specs=[hbm] * 6,
        out_specs=hbm,
        scratch_shapes=[
            pltpu.VMEM((4, 8, 2, LN, DH), F32),
            pltpu.VMEM((2, 16, LN, DH), F32),
            pltpu.VMEM((2048, 512), BF),
            pltpu.VMEM((2048, 768), BF),
            pltpu.VMEM((256, 2048), BF),
            pltpu.VMEM((256, 2048), BF),
            pltpu.VMEM((2048, 512), BF),
            pltpu.VMEM((2048, 768), BF),
            pltpu.VMEM((16, 280, LN), F32),
            pltpu.VMEM((2, 3, 7, 96, LN), F32),
            pltpu.VMEM((2, 2, LN, DH), F32),
            dma((6,)), dma((6,)), dma((6,)),
            dma((16,)), dma((16,)), dma((48,)), dma((48,)),
            dma((16,)), dma((16,)), dma((42,)), dma((42,)),
            dma((2,)), dma((2,)), dma((2,)),
        ],
        compiler_params=pltpu.CompilerParams(
            collective_id=0, has_side_effects=True, vmem_limit_bytes=62 << 20
        ),
        name="attention_tangent",
    )(queries, query_tangent, keys, key_tangent, values, value_tangent)
    return both[0], both[1]


def solution(mesh):
    spec = P(("pb", "kv"), None)
    return jax.shard_map(
        per_device, mesh=mesh, in_specs=(spec,) * 6, out_specs=(spec, spec), check_vma=False
    )
```
